32 devices in a mesh: row: 4 (over z), col: 8 (over y, x, core).
Axes of the slice: x: 2, y: 2, z: 4, core: 2. Of those that a mesh axis runs over, the one named last changes fastest.
Arguments:
- trace: float32 [16, 4, 8, 8, 128, 128], P(None, 'row', None, 'col'), may hold values from -6 to 6
- fill: int32 [16, 4, 8, 8], P(None, 'row', None, 'col'), may hold values 0 or 1
- pivots: float32 [2, 128, 128], replicated, may hold values from -0.046875 to 0.046875
- direct_rhs: float32 [16, 4, 16, 128], P(None, 'row'), may hold values from -6 to 6
- adjoint_rhs: float32 [16, 4, 16, 128], P(None, 'row'), may hold values from -6 to 6
Outputs:
- factored: float32 [16, 4, 8, 8, 128, 128], P(None, 'row', None, 'col')
- direct: float32 [16, 4, 16, 128], P(None, 'row')
- adjoint: float32 [16, 4, 16, 128], P(None, 'row')
- image: float32 [16, 4, 16, 128], P(None, 'row', 'col')
- back_image: float32 [8, 8, 16, 128], P(None, 'col', 'row')
The draws below stay inside these ranges and needn't reach their ends.
All inputs are finite; a program needn't handle non-finite values. No bound on the sum of `fill` on one device may be relied on, other than what follows from the above.
Results may differ from the reference program's by a relative error of at most 0.0003.
Values sent between devices are 32-bit elements; how exact they have to be, the bound alone decides.
A program may use at most 128 MiB of HBM per device.

```python
import jax
import jax.numpy as jnp
from jax import lax

BLOCK = 128
RB = 16
MODES = 16
CB = 8
NB = 64
N_ROW = 4
N_COL = 8


def set_ends(entries, key, least, top_value):
    longest = entries.shape.index(max(entries.shape))
    spots = []
    for shift in (0, 1):
        where = [jax.random.randint(jax.random.fold_in(key, axis), (), 0, length) for axis, length in enumerate(entries.shape)]
        where[longest] = (where[longest] + shift) % entries.shape[longest]
        spots.append(tuple(where))
    return entries.at[spots[0]].set(least).at[spots[1]].set(top_value)


def block_levels(rng, shape, cuts, smallest, largest):
    gain = 1.0
    for dim, blocks in cuts:
        draws = jax.random.uniform(jax.random.fold_in(jax.random.fold_in(rng, 6), dim), (blocks,), jnp.float32, smallest / len(cuts), largest / len(cuts))
        gain = gain * jnp.repeat(jnp.exp(draws), shape[dim] // blocks).reshape((-1,) + (1,) * (len(shape) - 1 - dim))
    return gain


def normal_values(rng, shape, deviation, bound, cuts=(), kind=jnp.bfloat16):
    entries = jax.random.normal(rng, shape, jnp.float32) * deviation
    if len(cuts) > 0:
        entries = block_levels(rng, shape, cuts, -0.22, 0.18) * entries
    return jnp.clip(entries, min=-bound, max=bound).astype(kind)


def setup_inputs(seed: int = 0) -> dict:
    key_of = jax.random.split(jax.random.key(seed), 6)
    return {
        "trace": normal_values(key_of[0], (RB, N_ROW, CB, N_COL, BLOCK, BLOCK), 1.0, 6.0, ((1, 4), (3, 8)), jnp.float32),
        "fill": set_ends((jax.random.randint(key_of[1], (RB, N_ROW, CB, N_COL), 0, 4) < 3).astype(jnp.int32), jax.random.fold_in(key_of[1], 1), 0, 1),
        "pivots": normal_values(key_of[2], (2, BLOCK, BLOCK), (BLOCK * BLOCK) ** -0.5, 0.046875, (), jnp.float32),
        "direct_rhs": normal_values(key_of[3], (RB, N_ROW, MODES, BLOCK), 1.0, 6.0, ((1, 4),), jnp.float32),
        "adjoint_rhs": normal_values(key_of[4], (RB, N_ROW, MODES, BLOCK), 1.0, 6.0, ((1, 4),), jnp.float32),
    }


def reference(trace, fill, pivots, direct_rhs, adjoint_rhs):
    highest = lax.Precision.HIGHEST
    blocks = (trace * fill[:, :, :, :, None, None].astype(jnp.float32)).reshape(NB, NB, BLOCK, BLOCK)
    order = jnp.arange(NB)
    for panel in range(2):
        below = order > panel
        formed = jnp.einsum('iab,bc->iac', blocks[:, panel], pivots[panel], precision=highest)
        lower = jnp.where(below[:, None, None], formed, blocks[:, panel])
        upper = blocks[panel]

        def update_row(item, upper=upper, panel=panel):
            row_blocks, lower_block, flag = item
            change = jnp.einsum('ab,jbc->jac', lower_block, upper, precision=highest)
            keep = (flag & (order > panel))[:, None, None]
            row_blocks = row_blocks - jnp.where(keep, change, 0.0)
            return row_blocks.at[panel].set(lower_block)

        blocks = lax.map(update_row, (blocks, lower, below))
    solution = direct_rhs.reshape(NB, MODES, BLOCK)
    for panel in range(2):
        column = jnp.where((order > panel)[:, None, None], blocks[:, panel], 0.0)
        solution = solution - jnp.einsum('iab,mb->ima', column, solution[panel], precision=highest)
    adjoint = adjoint_rhs.reshape(NB, MODES, BLOCK)
    for panel in (1, 0):
        column = jnp.where((order > panel)[:, None, None], blocks[:, panel], 0.0)
        adjoint = adjoint.at[panel].add(-jnp.einsum('iab,ima->mb', column, adjoint, precision=highest))
    scale = (NB * BLOCK) ** -0.5
    image = jnp.einsum('ijab,jmb->ima', blocks, solution, precision=highest) * scale
    back = jnp.einsum('ijab,ima->jmb', blocks, adjoint, precision=highest) * scale
    return (blocks.reshape(RB, N_ROW, CB, N_COL, BLOCK, BLOCK),
            solution.reshape(RB, N_ROW, MODES, BLOCK),
            adjoint.reshape(RB, N_ROW, MODES, BLOCK),
            image.reshape(RB, N_ROW, MODES, BLOCK),
            back.reshape(CB, N_COL, MODES, BLOCK))
```

```python
import functools

import jax
import jax.numpy as jnp
from jax import lax
from jax.experimental import pallas as pl
from jax.experimental.pallas import tpu as pltpu
from jax.sharding import PartitionSpec as P

F32 = jnp.float32
BF16 = jnp.bfloat16
NN = (((1,), (0,)), ((), ()))
NT = (((1,), (1,)), ((), ()))
MESH = pl.DeviceIdType.MESH


def split(x):
    high = x.astype(BF16)
    return high, (x - high.astype(F32)).astype(BF16)


def mul(a, b, dims=NN):
    return lax.dot_general(a, b, dims, preferred_element_type=F32)


def mul3(ah, al, bh, bl, dims=NN):
    return mul(ah, bh, dims) + mul(ah, bl, dims) + mul(al, bh, dims)


def stack(x):
    high, low = split(x)
    return jnp.concatenate([high, low], axis=0)


def thin(pair, bh, bl, dims=NN):
    half = pair.shape[0] // 2
    both = mul(pair, bh, dims)
    return both[:half] + both[half:] + mul(pair[:half], bl, dims)


def comm_kernel(
    n_row, n_col, trace, fill, pivots, direct, adjoint,
    fact, y_out, z_out, image, back,
    colbuf, rowbuf, small, drv, arv, piv, flags, cflag, rflag, kflag, cexp, rexp,
    mh, ml, lh, ll, wh, wl, kh, kl, l10, uh, ul, first, zst, yst, ysel, ycut,
    backp, sloc, sbuf, stot, ssib, zmsg, ximg, x0t, x0r, vloc, vbuf,
    img_t, img_r, back_t, back_r,
    load, local, cf_send, cf_recv, rf_send, rf_recv, sm_send, sm_recv,
    kz_send, kz_recv, kf_send, kf_recv, corner_send, corner_recv,
    ring_send, ring_recv, sib_send, sib_recv, row_up, row_down, row_recv,
    s_send, s_recv, ss_send, ss_recv, z_send, z_recv, y_send, y_recv,
    x_send, x_recv, v_send, v_recv, is_send, is_recv, bs_send, bs_recv,
):
    rows, cols, width = fact.shape[0], fact.shape[1], fact.shape[2]
    modes = y_out.shape[1]
    mi, mb = modes // n_col, modes // n_row
    scale = (rows * n_row * width) ** (-0.5)
    p = lax.axis_index("row")
    q = lax.axis_index("col")
    chips = n_col // 2
    deep = chips // 2
    chip, core = q // 2, q % 2
    cy, cx = chip // 2, chip % 2
    pos = cx * (cy + 1) + (1 - cx) * ((chips - cy) % chips)
    half = rows // 2
    group = rows // 4
    last = n_row - 1
    head = q < 2
    pf = p.astype(F32)

    def at_pos(r):
        side = 1 - ((r + chips - 1) % chips) // deep
        return (side * ((r - 1) * 2 + 1) + (1 - side) * (((chips - r) % chips) * 2)) * 2 + core

    after = at_pos((pos + 1) % chips)
    before = at_pos((pos + chips - 1) % chips)
    sibling = chip * 2 + 1 - core
    up = (p + 1) % n_row
    down = (p + n_row - 1) % n_row
    drains = []

    def to(src, dst, send, recv, row, col):
        return pltpu.make_async_remote_copy(
            src_ref=src, dst_ref=dst, send_sem=send, recv_sem=recv,
            device_id=(row, col), device_id_type=MESH,
        )

    def send(copy):
        copy.start()

    def when(cond, *fs):
        @pl.when(cond)
        def _():
            for f in fs:
                f()

    barrier = pltpu.get_barrier_semaphore()
    for d in range(1, n_col):
        pl.semaphore_signal(barrier, inc=1, device_id=(p, (q + d) % n_col), device_id_type=MESH)
    for d in range(1, n_row):
        pl.semaphore_signal(barrier, inc=1, device_id=((p + d) % n_row, q), device_id_type=MESH)

    loads = [
        pltpu.make_async_copy(fill, flags, local.at[0]),
        pltpu.make_async_copy(adjoint, arv, local.at[1]),
        pltpu.make_async_copy(direct, drv, local.at[2]),
        pltpu.make_async_copy(pivots, piv, local.at[3]),
    ]
    for x in loads:
        x.start()
    bulk = [
        pltpu.make_async_copy(trace.at[pl.ds(g * group, group)], fact.at[pl.ds(g * group, group)], load.at[g])
        for g in range(4)
    ]
    for x in bulk:
        x.start()
    slot = lax.rem(p, 2)
    own_row = [
        pltpu.make_async_copy(trace.at[0], rowbuf.at[slot], local.at[4]),
        pltpu.make_async_copy(direct.at[0], small.at[slot, 0], local.at[5]),
        pltpu.make_async_copy(adjoint.at[0], small.at[slot, 1], local.at[6]),
        pltpu.make_async_copy(fill, rflag.at[slot], local.at[7]),
    ]
    own_col = [
        pltpu.make_async_copy(trace.at[:, 0], colbuf.at[core, pl.ds(0, rows)], local.at[8]),
        pltpu.make_async_copy(fill, cflag.at[core], local.at[9]),
    ]
    own_corner = pltpu.make_async_copy(trace.at[0, 0], colbuf.at[core, rows], local.at[10])
    when(p < 2, *[x.start for x in own_row])
    when(head, *[x.start for x in own_col])
    when(head & (p == 1 - core), own_corner.start)

    pl.semaphore_wait(barrier, n_col + n_row - 2)

    def cf_copy(d):
        return to(fill, cflag.at[core], cf_send.at[d], cf_recv.at[core], p, (q + d) % n_col)

    def rf_copy(d):
        return to(fill, rflag.at[slot], rf_send.at[d], rf_recv.at[slot], (p + d) % n_row, q)

    def sm_copy(kind, d):
        src = (direct, adjoint)[kind].at[0]
        return to(src, small.at[slot, kind], sm_send.at[kind, d], sm_recv.at[slot, kind], (p + d) % n_row, q)

    def kz_copy(d):
        return to(trace.at[0, 0], colbuf.at[core, rows], kz_send.at[d], kz_recv, (p + d) % n_row, q)

    when(head & (p == 1 - core), *[kz_copy(d).start for d in range(1, n_row)])
    drains.append((head & (p == 1 - core), [kz_copy(d).wait_send for d in range(1, n_row)]))
    smalls = [rf_copy(d) for d in range(1, n_row)]
    smalls += [sm_copy(kind, d) for d in range(1, n_row) for kind in range(2)]
    when(p < 2, *[x.start for x in smalls])
    drains.append((p < 2, [x.wait_send for x in smalls]))
    plane = [cf_copy(d) for d in range(1, n_col)]
    when(head, *[x.start for x in plane])
    drains.append((head, [x.wait_send for x in plane]))

    def ring(block, dest):
        ref = colbuf.at[core, block]
        return to(ref, ref, ring_send.at[block], ring_recv.at[block], p, dest)

    def ring_first(block, dest):
        return to(trace.at[block, 0], colbuf.at[core, block], ring_send.at[block], ring_recv.at[block], p, dest)

    def sib(block, which):
        ref = colbuf.at[which, block]
        return to(ref, ref, sib_send.at[block], sib_recv.at[block], p, sibling)

    def sib_first(block):
        return to(trace.at[block, 0], colbuf.at[core, block], sib_send.at[block], sib_recv.at[block], p, sibling)

    def ring_step(k):
        if k < half:
            if k >= 2:
                when(head, ring(2 * k - 4, after).wait_send, ring(2 * k - 3, before).wait_send)
            when(
                head, ring_first(2 * k, after).start, ring_first(2 * k + 1, before).start,
                sib_first(2 * k).start, sib_first(2 * k + 1).start,
            )
        for forward in (True, False):
            s = k - 2 * (pos if forward else chips - pos)
            block = 2 * s + (0 if forward else 1)
            dest = after if forward else before
            stop = chips - 1 if forward else 1

            @pl.when((pos != 0) & (s >= 0) & (s < half))
            def _(block=block, dest=dest, stop=stop):
                ring(block, dest).wait_recv()
                when(pos != stop, ring(block, dest).start)
                sib(block, core).start()

    def row_copy(k, c, upward, own=False):
        src = trace.at[0, c] if own else rowbuf.at[k, c]
        sems = row_up if upward else row_down
        return to(src, rowbuf.at[k, c], sems.at[k, c], row_recv.at[k, c], up if upward else down, q)

    lag = max(0, 2 * (n_row - 3))

    def present(c):
        return (q >= 2) if c == 0 else (q >= 0)

    def row_step(k):
        if k < cols:
            if k >= 2:
                when((p == 0) & present(k - 2), row_copy(0, k - 2, True).wait_send)
            when((p == 0) & present(k), row_copy(0, k, True, True).start)
            when((p == 1) & present(k), row_copy(1, k, False, True).start)
        if n_row == 2:
            return
        if k < 2 * cols:
            if k >= 2:
                i = k - 2
                kk, c = (1, i) if i < cols else (0, i - cols)
                when((p == 1) & present(c), row_copy(kk, c, True).wait_send)
            if k < cols:
                when((p == 1) & present(k), row_copy(1, k, True, True).start)
            else:
                c = k - cols
                when((p == 1) & present(c), row_copy(0, c, True).wait_recv, row_copy(0, c, True).start)
        if n_row > 3:
            i = k - 2 * (p - 1)
            kk = jnp.where(i < cols, 1, 0)
            c = lax.rem(i, cols)

            @pl.when((p >= 2) & (p < last) & (i >= 0) & (i < 2 * cols) & ((c > 0) | (q >= 2)))
            def _():
                copy = row_copy(kk, c, True)
                copy.wait_recv()
                copy.start()

    def row_arrive(c):
        for k in range(2):
            passes = (p > k) & (p + 1 < n_row)
            when((p != k) & jnp.logical_not(passes) & present(c), row_copy(k, c, True).wait_recv)

    def corner(forward, dest):
        ref = colbuf.at[core, rows]
        return to(ref, ref, corner_send.at[0 if forward else 1], corner_recv.at[0], p, dest)

    def corner_sib(which):
        ref = colbuf.at[which, rows]
        return to(ref, ref, corner_send.at[2], corner_recv.at[1], p, sibling)

    def kf_copy(d):
        return to(rflag.at[1 - core], kflag.at[core], kf_send.at[d], kf_recv.at[core], p, (q + d) % n_col)

    def corner_step(k):
        if k == 2:
            when(head & (p == 1 - core), own_corner.wait, own_row[3].wait)
            when(head & (p != 1 - core), kz_copy(0).wait_recv, to(fill, rflag.at[1 - core], rf_send.at[0], rf_recv.at[1 - core], p, sibling).wait_recv)
            when(
                head, corner(True, after).start, corner(False, before).start, corner_sib(core).start,
                *[kf_copy(d).start for d in range(1, n_col)],
            )
            drains.append((head, [corner(True, after).wait_send, corner(False, before).wait_send, corner_sib(core).wait_send]))
            drains.append((head, [kf_copy(d).wait_send for d in range(1, n_col)]))

            @pl.when(head)
            def _():
                kflag[core] = rflag[1 - core]

        h = lax.div(k - 2, 2)
        if k > 2 and k % 2 == 0:
            hop = (k - 2) // 2
            if hop <= deep:
                @pl.when(pos == hop)
                def _():
                    corner(True, after).wait_recv()
                    if hop < deep:
                        corner(True, after).start()
                    corner_sib(core).start()

                if hop < deep:
                    drains.append((pos == hop, [corner(True, after).wait_send]))
                drains.append((pos == hop, [corner_sib(core).wait_send]))
            other = chips - hop
            if other > deep:
                @pl.when(pos == other)
                def _():
                    corner(False, before).wait_recv()
                    if other > deep + 1:
                        corner(False, before).start()
                    corner_sib(core).start()

                if other > deep + 1:
                    drains.append((pos == other, [corner(False, before).wait_send]))
                drains.append((pos == other, [corner_sib(core).wait_send]))

    corner_end = 2 + 2 * max(deep, chips - deep - 1)

    def comm(k):
        ring_step(k)
        corner_step(k)
        row_step(k)

    def start_flags():
        loads[0].wait()
        loads[1].wait()
        for a in range(rows):
            keep = jnp.where(p < 2, 0.0, 1.0) if a == 0 else 1.0
            h, l = split(arv[a] * keep)
            zst[0:modes, a * width:(a + 1) * width] = h
            zst[modes:2 * modes, a * width:(a + 1) * width] = l
        z_out[...] = arv[...]

    def piece_back(g):
        bulk[g].wait()
        for t in range(group):
            a = g * group + t
            for c in range(cols):
                h, l = split(fact[a, c] * flags[c, a].astype(F32))
                mh[a * width:(a + 1) * width, c * width:(c + 1) * width] = h
                ml[a * width:(a + 1) * width, c * width:(c + 1) * width] = l
        lo, n = g * group * width, group * width
        part = thin(zst[:, lo:lo + n], mh[lo:lo + n, :], ml[lo:lo + n, :])
        if g == 0:
            backp[...] = part
        else:
            backp[...] += part

    def s_copy(dest):
        return to(sloc, sbuf.at[p], s_send.at[dest], s_recv.at[p], dest, q)

    def send_s():
        @pl.when(head)
        def _():
            sloc[...] = backp[:, 0:width]
            for dest in range(2):
                when(p != dest, s_copy(dest).start)
            backp[:, 0:width] = jnp.zeros((modes, width), F32)

        for dest in range(2):
            drains.append((head & (p != dest), [s_copy(dest).wait_send]))

    def ss_copy():
        return to(stot, ssib, ss_send, ss_recv, p, sibling)

    def gather_s():
        @pl.when(head & (p < 2))
        def _():
            total = sloc[...]
            for r in range(n_row):
                when(p != r, to(sloc, sbuf.at[r], s_send.at[0], s_recv.at[r], p, sibling).wait_recv)
                total = total + jnp.where(p == r, 0.0, sbuf[r])
            stot[...] = total
            when(core == 1, ss_copy().start)

        drains.append((head & (p < 2) & (core == 1), [ss_copy().wait_send]))

    def z_copy(d):
        return to(zmsg, zmsg, z_send.at[d], z_recv, p, (q + d) % n_col)

    def solve_z():
        @pl.when((q == 0) & (p < 2))
        def _():
            ss_copy().wait_recv()
            w0 = thin(stack(stot[...]), kh[0], kl[0])
            w1 = thin(stack(ssib[...] - thin(stack(w0), kh[3], kl[3])), kh[1], kl[1])
            z1 = small[1, 1] - w1
            z1l = thin(stack(thin(stack(z1), kh[2], kl[2])), kh[0], kl[0])
            z0 = small[0, 1] - w0 - z1l
            a1 = z1 - w1
            a0 = z0 - w0 - thin(stack(thin(stack(a1), kh[2], kl[2])), kh[0], kl[0])
            zmsg[0] = jnp.where(p == 0, z0, z1)
            zmsg[1] = jnp.where(p == 0, a0, a1)
            zmsg[2] = z0 - z1l
            for d in range(1, n_col):
                z_copy(d).start()

        drains.append(((q == 0) & (p < 2), [z_copy(d).wait_send for d in range(1, n_col)]))

    def finish_back():
        @pl.when(p < 2)
        def _():
            when(q != 0, z_copy(0).wait_recv)
            z_out[0] = zmsg[0]
            a = zmsg[1]
            b = jnp.where(q == 0, jnp.where(p == 0, zmsg[0], 0.0), jnp.where(p == 0, zmsg[2], zmsg[0]))
            b = jnp.where(head, b, a)
            extra = jnp.where(p == q, small[slot, 1] - zmsg[0], 0.0)
            backp[:, 0:width] += thin(stack(b), mh[0:width, 0:width], ml[0:width, 0:width]) + extra
            backp[:, width:] += thin(stack(a), mh[0:width, width:], ml[0:width, width:])

        for c in range(cols):
            for m in range(modes):
                pass
        for c in range(cols):
            ximg[c] = backp[:, c * width:(c + 1) * width] * scale
        for m in range(modes):
            back_t[m] = ximg[0:cols, m, :]
        for d in range(1, n_row):
            back_copy(d).start()
        drains.append((None, [back_copy(d).wait_send for d in range(1, n_row)]))

    def back_copy(d):
        dest = (p + d) % n_row
        return to(back_t.at[pl.ds(dest * mb, mb)], back_r.at[p], bs_send.at[d], bs_recv.at[p], dest, q)

    def collect_back():
        total = back_t[pl.ds(p * mb, mb)]
        for d in range(1, n_row):
            peer = (p + d) % n_row
            to(back_r.at[peer], back_r.at[peer], bs_send.at[d], bs_recv.at[peer], peer, q).wait_recv()
            total = total + back_r[peer]
        for m in range(mb):
            back[:, m, :] = total[m]

    def form_flags():
        for k in range(2):
            when(head & (core == k), own_col[1].wait)
            when(jnp.logical_not(head & (core == k)), to(fill, cflag.at[k], cf_send.at[0], cf_recv.at[k], p, sibling).wait_recv)
            when(p == k, own_row[1].wait, own_row[2].wait)
            when(p != k, *[to(small.at[k, x], small.at[k, x], sm_send.at[x, 0], sm_recv.at[k, x], p, sibling).wait_recv for x in range(2)])
            when((p == k) & jnp.logical_not(head & (core == 1 - k)), own_row[3].wait)
            when((p != k) & jnp.logical_not(head & (core == 1 - k)), to(fill, rflag.at[k], rf_send.at[0], rf_recv.at[k], p, sibling).wait_recv)
            when(jnp.logical_not(head & (core == k)), to(rflag.at[0], kflag.at[k], kf_send.at[0], kf_recv.at[k], p, sibling).wait_recv)
        corner_sib(1 - core).wait_recv()
        when(p < 2, own_row[0].wait)
        loads[2].wait()
        loads[3].wait()
        when(head, own_col[0].wait)

        @pl.when(head)
        def _():
            for k in range(2):
                rowbuf[k, 0] = jnp.zeros((width, width), F32)

        eye = (lax.broadcasted_iota(jnp.int32, (rows, rows), 0) == lax.broadcasted_iota(jnp.int32, (rows, rows), 1)).astype(F32)
        for k in range(2):
            line = cflag[k, 0:1, :].astype(F32)
            cexp[k] = jnp.broadcast_to(jnp.sum(line * eye, axis=1, keepdims=True), (rows, width))
            rexp[k] = jnp.broadcast_to(rflag[k, :, 0:1].astype(F32), (cols, width))
        for k in range(2):
            h, l = split(piv[k])
            kh[k] = h
            kl[k] = l
            h, l = split(colbuf[k, rows] * kflag[k, 0:1, 0:1].astype(F32))
            kh[2 + k] = h
            kl[2 + k] = l
        lower = mul3(kh[2], kl[2], kh[0], kl[0])
        h, l = split(lower)
        l10[0] = h
        l10[1] = l
        eh, el = split(mul3(kh[0], kl[0], kh[3], kl[3]))
        th, tl = split(-mul3(eh, el, kh[1], kl[1]))
        wh[0:width, 0:width] = kh[0]
        wl[0:width, 0:width] = kl[0]
        wh[0:width, width:] = th
        wl[0:width, width:] = tl
        wh[width:, 0:width] = jnp.zeros((width, width), BF16)
        wl[width:, 0:width] = jnp.zeros((width, width), BF16)
        wh[width:, width:] = kh[1]
        wl[width:, width:] = kl[1]
        y1 = small[1, 0] - thin(stack(small[0, 0]), h, l, NT)
        for k, y in ((0, small[0, 0]), (1, y1)):
            h, l = split(y)
            yst[0:modes, k * width:(k + 1) * width] = h
            yst[modes:, k * width:(k + 1) * width] = l
            for d in range(n_col):
                ycut[k, d] = y[d * mi:(d + 1) * mi]

    def form(g):
        for t in range(group):
            sib(g * group + t, 1 - core).wait_recv()
        blocks = []
        for t in range(group):
            a = g * group + t
            blocks.append(jnp.concatenate([colbuf[k, a] * cexp[k, a:a + 1, :] for k in range(2)], axis=1))
        h, l = split(jnp.concatenate(blocks, axis=0))
        lower = mul3(h, l, wh[...], wl[...])
        if g == 0:
            m0 = jnp.where(p > 0, 1.0, 0.0)
            m1 = jnp.where(p > 1, 1.0, 0.0)
            l0 = lower[0:width, 0:width] * m0
            l1 = lower[0:width, width:] * m1
            xh, xl = split(l0)
            mid = blocks[0][:, width:] - mul3(xh, xl, kh[3], kl[3])
            first[:, 0:width] = jnp.where(p > 0, l0, blocks[0][:, 0:width])
            first[:, width:] = jnp.where(p > 1, l1, mid)
            lower = jnp.concatenate([jnp.concatenate([l0, l1], axis=1), lower[width:]], axis=0)
        for k in range(2):
            @pl.when(q == k)
            def _(k=k):
                for t in range(group):
                    a = g * group + t
                    if a == 0:
                        fact[a, 0] = first[:, k * width:(k + 1) * width]
                    else:
                        fact[a, 0] = lower[t * width:(t + 1) * width, k * width:(k + 1) * width]
        h, l = split(lower)
        lo, n = g * group * width, group * width
        lh[lo:lo + n, :] = h
        ll[lo:lo + n, :] = l
        change = thin(yst[:, 0:2 * width], h, l, NT)
        for t in range(group):
            a = g * group + t
            y_out[a] = drv[a] - change[:, t * width:(t + 1) * width]

    owner = q % n_row
    step = n_col // n_row

    def y_copy(d):
        return to(ysel, ysel, y_send.at[d], y_recv, (p + d) % n_row, q)

    def send_y():
        @pl.when(p == owner)
        def _():
            for c in range(cols):
                ysel[c] = y_out[c * step + q // n_row]
            for d in range(1, n_row):
                y_copy(d).start()

        drains.append((p == owner, [y_copy(d).wait_send for d in range(1, n_row)]))

    def take_y():
        when(p != owner, to(ysel, ysel, y_send.at[0], y_recv, p, sibling).wait_recv)
        for c in range(cols):
            keep = jnp.where(head, 0.0, 1.0) if c == 0 else 1.0
            h, l = split(ysel[c] * keep)
            yst[0:modes, c * width:(c + 1) * width] = h
            yst[modes:, c * width:(c + 1) * width] = l

    def piece_image(g):
        lo, n = g * group * width, group * width
        part = thin(yst[...], mh[lo:lo + n, :], ml[lo:lo + n, :], NT)
        for t in range(group):
            ximg[g * group + t] = part[:, t * width:(t + 1) * width]

    def x_copy(d):
        dest = (q + d) % n_col
        return to(x0t.at[dest], x0r.at[q], x_send.at[d], x_recv.at[q], p, dest)

    def send_x0():
        @pl.when(p < 2)
        def _():
            for d in range(n_col):
                x0t[d] = ximg[0, d * mi:(d + 1) * mi, :]
            for d in range(1, n_col):
                x_copy(d).start()

        drains.append((p < 2, [x_copy(d).wait_send for d in range(1, n_col)]))

    def v_copy(d):
        return to(vloc, vbuf.at[slot], v_send.at[d], v_recv.at[slot], (p + d) % n_row, q)

    def send_v():
        @pl.when(p < 2)
        def _():
            total = x0t[q]
            for d in range(1, n_col):
                peer = (q + d) % n_col
                to(x0r.at[peer], x0r.at[peer], x_send.at[d], x_recv.at[peer], p, peer).wait_recv()
                total = total + x0r[peer]
            vloc[...] = total
            vbuf[slot] = total
            for d in range(1, n_row):
                v_copy(d).start()

        drains.append((p < 2, [v_copy(d).wait_send for d in range(1, n_row)]))

    def img_copy(d):
        dest = (q + d) % n_col
        return to(img_t.at[pl.ds(dest * mi, mi)], img_r.at[q], is_send.at[d], is_recv.at[q], p, dest)

    def send_image():
        for m in range(modes):
            img_t[m] = ximg[:, m, :]
        for d in range(1, n_col):
            img_copy(d).start()
        drains.append((None, [img_copy(d).wait_send for d in range(1, n_col)]))

    def collect_image():
        for k in range(2):
            when(p != k, to(vbuf.at[k], vbuf.at[k], v_send.at[0], v_recv.at[k], p, sibling).wait_recv)
        x0 = vbuf[0]
        pad = jnp.zeros((8 - mi, width), F32)
        v1 = vbuf[1] - thin(stack(jnp.concatenate([x0, pad], axis=0)), l10[0], l10[1], NT)[0:mi]
        y0, y1 = ycut[0, q], ycut[1, q]
        wide = jnp.zeros((8 - mi, 2 * width), F32)

        def padded(g0, g1):
            return stack(jnp.concatenate([jnp.concatenate([g0, g1], axis=1), wide], axis=0))

        fix = thin(padded(y0 - x0, y1 - v1), lh[...], ll[...], NT)
        g0 = y0 - jnp.where(p > 0, x0, 0.0)
        g1 = y1 - jnp.where(p > 1, v1, 0.0)
        fh, fl = split(first[...])
        head_fix = thin(padded(g0, g1), fh, fl, NT)
        total = img_t[pl.ds(q * mi, mi)]
        for d in range(1, n_col):
            peer = (q + d) % n_col
            to(img_r.at[peer], img_r.at[peer], is_send.at[d], is_recv.at[peer], p, peer).wait_recv()
            total = total + img_r[peer]
        for a in range(rows):
            change = head_fix if a == 0 else fix[:, a * width:(a + 1) * width]
            image[a] = (total[:, a, :] + change[0:mi]) * scale

    def update(c):
        row_arrive(c)
        row_arrive(c + 1)
        u0 = jnp.concatenate([rowbuf[0, x] * rexp[0, x:x + 1, :] for x in (c, c + 1)], axis=1)
        u1 = jnp.concatenate([rowbuf[1, x] * rexp[1, x:x + 1, :] for x in (c, c + 1)], axis=1)
        h0, l0 = split(u0)
        h1, l1 = split(u1 - mul3(l10[0], l10[1], h0, l0))
        uh[0:width, :] = h0
        ul[0:width, :] = l0
        uh[width:, :] = h1
        ul[width:, :] = l1
        change = mul3(lh[...], ll[...], uh[...], ul[...])
        for a in range(rows):
            for e in range(2):
                value = fact[a, c + e] * flags[c + e, a].astype(F32)
                value = value - change[a * width:(a + 1) * width, e * width:(e + 1) * width]
                if c + e == 0:
                    value = jnp.where(head, fact[a, 0], value)
                fact[a, c + e] = value

    ring_end = half - 1 + 2 * (chips - 1)
    ticks = max(2 * cols + lag, ring_end + 1, corner_end + 1)
    plan = {}

    def at(k, *fs):
        plan.setdefault(min(k, ticks), []).extend(fs)

    at(0, start_flags, lambda: piece_back(0))
    at(1, lambda: piece_back(1))
    at(2, lambda: piece_back(2))
    at(3, lambda: piece_back(3), send_s)
    at(corner_end + 1, form_flags)
    for g in range(4):
        at((g + 1) * group // 2 - 1 + 2 * (chips - 1) + 1, lambda g=g: form(g))
    at(ring_end - 3, gather_s)
    at(ring_end - 2, solve_z)
    at(ring_end + 1, send_y)
    at(ring_end + 1, finish_back)
    upd = [(c, cols + c + 1 + lag) for c in range(0, cols, 2)]
    at(max(upd[0][1], ring_end + 2), lambda: update(0))
    at(ring_end + 3, take_y, lambda: piece_image(0), send_x0, lambda: piece_image(1))
    at(ring_end + 3, lambda: piece_image(2), lambda: piece_image(3), send_image)
    for c, k in upd[1:-1]:
        at(max(k, ring_end + 4), lambda c=c: update(c))
    for k in range(ticks):
        comm(k)
        for f in plan.get(k, ()):
            f()
    for f in plan.get(ticks, ()):
        f()
    send_v()
    update(cols - 2)
    collect_back()
    collect_image()

    for cond, fs in drains:
        if cond is None:
            for f in fs:
                f()
        else:
            when(cond, *fs)
    for block in range(rows):
        stop = chips - 1 if block % 2 == 0 else 1
        due = (pos != 0) & (pos != stop)
        if block >= rows - 4:
            due = due | (pos == 0)
        when(due, ring(block, after).wait_send)
        sib(block, core).wait_send()
    for c in range(cols):
        when((p == 1) & present(c), row_copy(1, c, False).wait_send)
        if c >= cols - 2:
            when((p == 0) & present(c), row_copy(0, c, True).wait_send)
            if n_row > 2:
                when((p == 1) & present(c), row_copy(0, c, True).wait_send)
        if n_row > 3:
            for k in range(2):
                when((p >= 2) & (p < last) & present(c), row_copy(k, c, True).wait_send)


def store_kernel(fact, y, z, img, bck, out, y_out, z_out, img_out, bck_out, sems):
    parts = 8
    n = fact.shape[0] // parts
    copies = [
        pltpu.make_async_copy(fact.at[pl.ds(i * n, n)], out.at[pl.ds(i * n, n)], sems.at[i]) for i in range(parts)
    ]
    for i, (src, dst) in enumerate(((y, y_out), (z, z_out), (img, img_out), (bck, bck_out))):
        copies.append(pltpu.make_async_copy(src, dst, sems.at[parts + i]))
    for copy in copies:
        copy.start()
    for copy in copies:
        copy.wait()


def shards(trace, fill, pivots, direct_rhs, adjoint_rhs):
    n_row, n_col = lax.axis_size("row"), lax.axis_size("col")
    rows, cols, width = trace.shape[0], trace.shape[2], trace.shape[4]
    modes = direct_rhs.shape[2]
    blocks = trace.reshape(rows, cols, width, width)
    flags = fill.reshape(rows, cols).T
    mi, mb = modes // n_col, modes // n_row
    hbm = pl.BlockSpec(memory_space=pltpu.HBM)
    vmem = pl.BlockSpec(memory_space=pltpu.VMEM)
    shape = jax.ShapeDtypeStruct
    dma = pltpu.SemaphoreType.DMA
    V = pltpu.VMEM
    outs = pl.pallas_call(
        functools.partial(comm_kernel, n_row, n_col),
        out_shape=(
            shape((rows, cols, width, width), F32),
            shape((rows, modes, width), F32),
            shape((rows, modes, width), F32),
            shape((rows, mi, width), F32),
            shape((cols, mb, width), F32),
        ),
        in_specs=[hbm] * 5,
        out_specs=[vmem] * 5,
        scratch_shapes=[
            V((2, rows + 1, width, width), F32),
            V((2, cols, width, width), F32),
            V((2, 2, modes, width), F32),
            V((rows, modes, width), F32),
            V((rows, modes, width), F32),
            V((2, width, width), F32),
            pltpu.SMEM((cols, rows), jnp.int32),
            V((2, cols, rows), jnp.int32),
            V((2, cols, rows), jnp.int32),
            V((2, cols, rows), jnp.int32),
            V((2, rows, width), F32),
            V((2, cols, width), F32),
            V((rows * width, cols * width), BF16),
            V((rows * width, cols * width), BF16),
            V((rows * width, 2 * width), BF16),
            V((rows * width, 2 * width), BF16),
            V((2 * width, 2 * width), BF16),
            V((2 * width, 2 * width), BF16),
            V((4, width, width), BF16),
            V((4, width, width), BF16),
            V((2, width, width), BF16),
            V((2 * width, 2 * width), BF16),
            V((2 * width, 2 * width), BF16),
            V((width, 2 * width), F32),
            V((2 * modes, rows * width), BF16),
            V((2 * modes, cols * width), BF16),
            V((cols, modes, width), F32),
            V((2, n_col, mi, width), F32),
            V((modes, cols * width), F32),
            V((modes, width), F32),
            V((n_row, modes, width), F32),
            V((modes, width), F32),
            V((modes, width), F32),
            V((3, modes, width), F32),
            V((rows, modes, width), F32),
            V((n_col, mi, width), F32),
            V((n_col, mi, width), F32),
            V((mi, width), F32),
            V((2, mi, width), F32),
            V((modes, rows, width), F32),
            V((n_col, mi, rows, width), F32),
            V((modes, cols, width), F32),
            V((n_row, mb, cols, width), F32),
            dma((4,)), dma((11,)),
            dma((n_col,)), dma((2,)), dma((n_row,)), dma((2,)), dma((2, n_row)), dma((2, 2)),
            dma((n_row,)), dma, dma((n_col,)), dma((2,)), dma((3,)), dma((2,)),
            dma((rows,)), dma((rows,)), dma((rows,)), dma((rows,)),
            dma((2, cols)), dma((2, cols)), dma((2, cols)),
            dma((2,)), dma((n_row,)), dma, dma, dma((n_col,)), dma, dma((n_row,)), dma,
            dma((n_col,)), dma((n_col,)), dma((n_row,)), dma((2,)),
            dma((n_col,)), dma((n_col,)), dma((n_row,)), dma((n_row,)),
        ],
        compiler_params=pltpu.CompilerParams(
            collective_id=0, has_side_effects=True, vmem_limit_bytes=40 * 1024 * 1024
        ),
    )(*[pltpu.with_memory_space_constraint(x, pltpu.HBM) for x in (blocks, flags, pivots, direct_rhs[:, 0], adjoint_rhs[:, 0])])
    factored, direct, adjoint, image, back = pl.pallas_call(
        store_kernel,
        out_shape=tuple(shape(x.shape, F32) for x in outs),
        in_specs=[vmem] * 5,
        out_specs=[hbm] * 5,
        scratch_shapes=[dma((12,))],
        compiler_params=pltpu.CompilerParams(vmem_limit_bytes=16 * 1024 * 1024),
    )(*outs)
    return (
        factored[:, None, :, None],
        direct[:, None],
        adjoint[:, None],
        image[:, None],
        back[:, None],
    )


def solution(mesh):
    placed = (
        P(None, "row", None, "col", None, None),
        P(None, "row", None, "col"),
        P(),
        P(None, "row", None, None),
        P(None, "row", None, None),
    )
    return jax.shard_map(
        shards,
        mesh=mesh,
        in_specs=placed,
        out_specs=(
            P(None, "row", None, "col", None, None),
            P(None, "row", None, None),
            P(None, "row", None, None),
            P(None, "row", "col", None),
            P(None, "col", "row", None),
        ),
        check_vma=False,
    )
```

```python
import functools

import jax
import jax.numpy as jnp
from jax import lax
from jax.experimental import pallas as pl
from jax.experimental.pallas import tpu as pltpu
from jax.sharding import PartitionSpec as P

F32 = jnp.float32
BF16 = jnp.bfloat16
NN = (((1,), (0,)), ((), ()))
NT = (((1,), (1,)), ((), ()))
MESH = pl.DeviceIdType.MESH


def split(x):
    high = x.astype(BF16)
    return high, (x - high.astype(F32)).astype(BF16)


def mul(a, b, dims=NN):
    return lax.dot_general(a, b, dims, preferred_element_type=F32)


def mul3(ah, al, bh, bl, dims=NN):
    return mul(ah, bh, dims) + mul(ah, bl, dims) + mul(al, bh, dims)


def stack(x):
    high, low = split(x)
    return jnp.concatenate([high, low], axis=0)


def thin(pair, bh, bl, dims=NN):
    half = pair.shape[0] // 2
    both = mul(pair, bh, dims)
    return both[:half] + both[half:] + mul(pair[:half], bl, dims)


def comm_kernel(
    n_row, n_col, trace, fill, pivots, direct, adjoint,
    fact, y_out, z_out, image, back,
    colbuf, rowbuf, small, drv, arv, piv, flags, cflag, rflag, kflag, cexp, rexp,
    mh, ml, lh, ll, wh, wl, kh, kl, l10, uh, ul, first, zst, yst, ypair, ytop, ysel, yown, tcut, trecv, ycut,
    backp, sloc, sbuf, stot, ssib, zmsg, ximg, x0t, x0r, vloc, vbuf,
    img_t, img_r, back_t, back_r,
    load, local, cf_send, cf_recv, rf_send, rf_recv, sm_send, sm_recv,
    kz_send, kz_recv, kf_send, kf_recv, corner_send, corner_recv,
    ring_send, ring_recv, sib_send, sib_recv, row_up, row_down, row_recv,
    s_send, s_recv, ss_send, ss_recv, z_send, z_recv, y_send, y_recv, t_send, t_recv, yp_send, yp_recv,
    x_send, x_recv, v_send, v_recv, is_send, is_recv, bs_send, bs_recv,
):
    rows, cols, width = fact.shape[0], fact.shape[1], fact.shape[2]
    modes = y_out.shape[1]
    mi, mb = modes // n_col, modes // n_row
    scale = (rows * n_row * width) ** (-0.5)
    p = lax.axis_index("row")
    q = lax.axis_index("col")
    chips = n_col // 2
    deep = chips // 2
    chip, core = q // 2, q % 2
    cy, cx = chip // 2, chip % 2
    pos = cx * (cy + 1) + (1 - cx) * ((chips - cy) % chips)
    half = rows // 2
    group = rows // 4
    last = n_row - 1
    head = q < 2
    pf = p.astype(F32)

    def at_pos(r):
        side = 1 - ((r + chips - 1) % chips) // deep
        return (side * ((r - 1) * 2 + 1) + (1 - side) * (((chips - r) % chips) * 2)) * 2 + core

    after = at_pos((pos + 1) % chips)
    before = at_pos((pos + chips - 1) % chips)
    sibling = chip * 2 + 1 - core
    up = (p + 1) % n_row
    down = (p + n_row - 1) % n_row
    drains = []
    depth = 3
    met = 4

    def to(src, dst, send, recv, row, col):
        return pltpu.make_async_remote_copy(
            src_ref=src, dst_ref=dst, send_sem=send, recv_sem=recv,
            device_id=(row, col), device_id_type=MESH,
        )

    def send(copy):
        copy.start()

    def when(cond, *fs):
        @pl.when(cond)
        def _():
            for f in fs:
                f()

    barrier = pltpu.get_barrier_semaphore()
    for d in range(1, n_col):
        pl.semaphore_signal(barrier, inc=1, device_id=(p, (q + d) % n_col), device_id_type=MESH)
    for d in range(1, n_row):
        pl.semaphore_signal(barrier, inc=1, device_id=((p + d) % n_row, q), device_id_type=MESH)

    loads = [
        pltpu.make_async_copy(fill, flags, local.at[0]),
        pltpu.make_async_copy(adjoint, arv, local.at[1]),
        pltpu.make_async_copy(direct, drv, local.at[2]),
        pltpu.make_async_copy(pivots, piv, local.at[3]),
    ]
    for x in loads:
        x.start()
    bulk = [
        pltpu.make_async_copy(trace.at[pl.ds(g * group, group)], fact.at[pl.ds(g * group, group)], load.at[g])
        for g in range(4)
    ]
    for x in bulk:
        x.start()
    slot = lax.rem(p, 2)
    own_row = [
        pltpu.make_async_copy(trace.at[0], rowbuf.at[slot], local.at[4]),
        pltpu.make_async_copy(direct.at[0], small.at[slot, 0], local.at[5]),
        pltpu.make_async_copy(adjoint.at[0], small.at[slot, 1], local.at[6]),
        pltpu.make_async_copy(fill, rflag.at[slot], local.at[7]),
    ]
    own_col = [
        pltpu.make_async_copy(trace.at[:, 0], colbuf.at[core, pl.ds(0, rows)], local.at[8]),
        pltpu.make_async_copy(fill, cflag.at[core], local.at[9]),
    ]
    own_corner = pltpu.make_async_copy(trace.at[0, 0], colbuf.at[core, rows], local.at[10])
    when(p < 2, *[x.start for x in own_row])
    when(head, *[x.start for x in own_col])
    when(head & (p == 1 - core), own_corner.start)

    pl.semaphore_wait(barrier, n_col + n_row - 2)

    def cf_copy(d):
        return to(fill, cflag.at[core], cf_send.at[d], cf_recv.at[core], p, (q + d) % n_col)

    def rf_copy(d):
        return to(fill, rflag.at[slot], rf_send.at[d], rf_recv.at[slot], (p + d) % n_row, q)

    def sm_copy(kind, d):
        src = (direct, adjoint)[kind].at[0]
        return to(src, small.at[slot, kind], sm_send.at[kind, d], sm_recv.at[slot, kind], (p + d) % n_row, q)

    def kz_copy(d):
        return to(trace.at[0, 0], colbuf.at[core, rows], kz_send.at[d], kz_recv, (p + d) % n_row, q)

    when(head & (p == 1 - core), *[kz_copy(d).start for d in range(1, n_row)])
    drains.append((head & (p == 1 - core), [kz_copy(d).wait_send for d in range(1, n_row)]))
    smalls = [rf_copy(d) for d in range(1, n_row)]
    smalls += [sm_copy(kind, d) for d in range(1, n_row) for kind in range(2)]
    when(p < 2, *[x.start for x in smalls])
    drains.append((p < 2, [x.wait_send for x in smalls]))
    plane = [cf_copy(d) for d in range(1, n_col)]
    when(head, *[x.start for x in plane])
    drains.append((head, [x.wait_send for x in plane]))

    def ring(block, dest):
        ref = colbuf.at[core, block]
        return to(ref, ref, ring_send.at[block], ring_recv.at[block], p, dest)

    def ring_first(block, dest):
        return to(trace.at[block, 0], colbuf.at[core, block], ring_send.at[block], ring_recv.at[block], p, dest)

    def sib(block, which):
        ref = colbuf.at[which, block]
        return to(ref, ref, sib_send.at[block], sib_recv.at[block], p, sibling)

    def sib_first(block):
        return to(trace.at[block, 0], colbuf.at[core, block], sib_send.at[block], sib_recv.at[block], p, sibling)

    def ring_step(k):
        for j in range(min(depth, half)) if k == 0 else range(max(k, depth), min(k + 1, half)):
            if j >= depth:
                when(head, ring(2 * (j - depth), after).wait_send, ring(2 * (j - depth) + 1, before).wait_send)
            when(
                head, ring_first(2 * j, after).start, ring_first(2 * j + 1, before).start,
                sib_first(2 * j).start, sib_first(2 * j + 1).start,
            )
        for forward in (True, False):
            s = k - 2 * (pos if forward else chips - pos)
            block = 2 * s + (0 if forward else 1)
            dest = after if forward else before
            stop = chips - 1 if forward else 1

            @pl.when((pos != 0) & (s >= 0) & (s < half))
            def _(block=block, dest=dest, stop=stop):
                ring(block, dest).wait_recv()
                when(pos != stop, ring(block, dest).start)
                sib(block, core).start()

    def row_copy(k, c, upward, own=False):
        src = trace.at[0, c] if own else rowbuf.at[k, c]
        sems = row_up if upward else row_down
        return to(src, rowbuf.at[k, c], sems.at[k, c], row_recv.at[k, c], up if upward else down, q)

    lag = 8 + 2 * (n_row - 4) if n_row > 3 else 0

    def present(c):
        return (q >= 2) if c == 0 else (q >= 0)

    def row_step(k):
        if k == 0:
            for c in range(cols):
                when((p == 0) & present(c), row_copy(0, c, True, True).start)
                if n_row > 2:
                    when((p == 1) & present(c), row_copy(1, c, True, True).start)
                when((p == 1) & present(c), row_copy(1, c, False, True).start)
        if n_row > 2 and cols <= k < 2 * cols:
            c = k - cols
            when((p == 1) & present(c), row_copy(0, c, True).wait_recv, row_copy(0, c, True).start)
        if n_row > 3:
            i = k - 4 - 2 * (p - 2) - jnp.where(head, 4, 0)
            kk = jnp.where(i < cols, 1, 0)
            c = lax.rem(i, cols)

            @pl.when((p >= 2) & (p < last) & (i >= 0) & (i < 2 * cols) & ((c > 0) | (q >= 2)))
            def _():
                copy = row_copy(kk, c, True)
                copy.wait_recv()
                copy.start()

    def row_arrive(c):
        for k in range(2):
            passes = (p > k) & (p + 1 < n_row)
            when((p != k) & jnp.logical_not(passes) & present(c), row_copy(k, c, True).wait_recv)

    def corner(forward, dest):
        ref = colbuf.at[core, rows]
        return to(ref, ref, corner_send.at[0 if forward else 1], corner_recv.at[0], p, dest)

    def corner_sib(which):
        ref = colbuf.at[which, rows]
        return to(ref, ref, corner_send.at[2], corner_recv.at[1], p, sibling)

    def kf_copy(d):
        return to(rflag.at[1 - core], kflag.at[core], kf_send.at[d], kf_recv.at[core], p, (q + d) % n_col)

    def corner_step(k):
        if k == met:
            when(head & (p == 1 - core), own_corner.wait, own_row[3].wait)
            when(head & (p != 1 - core), kz_copy(0).wait_recv, to(fill, rflag.at[1 - core], rf_send.at[0], rf_recv.at[1 - core], p, sibling).wait_recv)
            when(
                head, corner(True, after).start, corner(False, before).start, corner_sib(core).start,
                *[kf_copy(d).start for d in range(1, n_col)],
            )
            drains.append((head, [corner(True, after).wait_send, corner(False, before).wait_send, corner_sib(core).wait_send]))
            drains.append((head, [kf_copy(d).wait_send for d in range(1, n_col)]))

            @pl.when(head)
            def _():
                kflag[core] = rflag[1 - core]

        if k > met + 1 and (k - met - 1) % 3 == 0:
            hop = (k - met - 1) // 3
            if hop <= deep:
                @pl.when(pos == hop)
                def _():
                    corner(True, after).wait_recv()
                    if hop < deep:
                        corner(True, after).start()
                    corner_sib(core).start()

                if hop < deep:
                    drains.append((pos == hop, [corner(True, after).wait_send]))
                drains.append((pos == hop, [corner_sib(core).wait_send]))
            other = chips - hop
            if other > deep:
                @pl.when(pos == other)
                def _():
                    corner(False, before).wait_recv()
                    if other > deep + 1:
                        corner(False, before).start()
                    corner_sib(core).start()

                if other > deep + 1:
                    drains.append((pos == other, [corner(False, before).wait_send]))
                drains.append((pos == other, [corner_sib(core).wait_send]))

    corner_end = met + 1 + 3 * max(deep, chips - deep - 1)

    def start_flags():
        loads[0].wait()
        loads[1].wait()
        for a in range(rows):
            keep = jnp.where(p < 2, 0.0, 1.0) if a == 0 else 1.0
            h, l = split(arv[a] * keep)
            zst[0:modes, a * width:(a + 1) * width] = h
            zst[modes:2 * modes, a * width:(a + 1) * width] = l
        z_out[...] = arv[...]

    def piece_back(g):
        bulk[g].wait()
        for t in range(group):
            a = g * group + t
            for c in range(cols):
                h, l = split(fact[a, c] * flags[c, a].astype(F32))
                mh[a * width:(a + 1) * width, c * width:(c + 1) * width] = h
                ml[a * width:(a + 1) * width, c * width:(c + 1) * width] = l
        lo, n = g * group * width, group * width
        part = thin(zst[:, lo:lo + n], mh[lo:lo + n, :], ml[lo:lo + n, :])
        if g == 0:
            backp[...] = part
        else:
            backp[...] += part

    def s_copy(dest):
        return to(sloc, sbuf.at[p], s_send.at[dest], s_recv.at[p], dest, q)

    def send_s():
        @pl.when(head)
        def _():
            sloc[...] = backp[:, 0:width]
            for dest in range(2):
                when(p != dest, s_copy(dest).start)
            backp[:, 0:width] = jnp.zeros((modes, width), F32)

        for dest in range(2):
            drains.append((head & (p != dest), [s_copy(dest).wait_send]))

    def ss_copy():
        return to(stot, ssib, ss_send, ss_recv, p, sibling)

    def gather_s():
        @pl.when(head & (p < 2))
        def _():
            total = sloc[...]
            for r in range(n_row):
                when(p != r, to(sloc, sbuf.at[r], s_send.at[0], s_recv.at[r], p, sibling).wait_recv)
                total = total + jnp.where(p == r, 0.0, sbuf[r])
            stot[...] = total
            when(core == 1, ss_copy().start)

        drains.append((head & (p < 2) & (core == 1), [ss_copy().wait_send]))

    def z_copy(d):
        return to(zmsg, zmsg, z_send.at[d], z_recv, p, (q + d) % n_col)

    def solve_z():
        @pl.when((q == 0) & (p < 2))
        def _():
            ss_copy().wait_recv()
            w0 = thin(stack(stot[...]), kh[0], kl[0])
            w1 = thin(stack(ssib[...] - thin(stack(w0), kh[3], kl[3])), kh[1], kl[1])
            z1 = small[1, 1] - w1
            z1l = thin(stack(thin(stack(z1), kh[2], kl[2])), kh[0], kl[0])
            z0 = small[0, 1] - w0 - z1l
            a1 = z1 - w1
            a0 = z0 - w0 - thin(stack(thin(stack(a1), kh[2], kl[2])), kh[0], kl[0])
            zmsg[0] = jnp.where(p == 0, z0, z1)
            zmsg[1] = jnp.where(p == 0, a0, a1)
            zmsg[2] = z0 - z1l
            for d in range(1, n_col):
                z_copy(d).start()

        drains.append(((q == 0) & (p < 2), [z_copy(d).wait_send for d in range(1, n_col)]))

    def finish_back():
        @pl.when(p < 2)
        def _():
            when(q != 0, z_copy(0).wait_recv)
            z_out[0] = zmsg[0]
            a = zmsg[1]
            b = jnp.where(q == 0, jnp.where(p == 0, zmsg[0], 0.0), jnp.where(p == 0, zmsg[2], zmsg[0]))
            b = jnp.where(head, b, a)
            extra = jnp.where(p == q, small[slot, 1] - zmsg[0], 0.0)
            backp[:, 0:width] += thin(stack(b), mh[0:width, 0:width], ml[0:width, 0:width]) + extra
            backp[:, width:] += thin(stack(a), mh[0:width, width:], ml[0:width, width:])

        for c in range(cols):
            for m in range(modes):
                pass
        for c in range(cols):
            ximg[c] = backp[:, c * width:(c + 1) * width] * scale
        for m in range(modes):
            back_t[m] = ximg[0:cols, m, :]
        for d in range(1, n_row):
            back_copy(d).start()

    def back_copy(d):
        dest = (p + d) % n_row
        return to(back_t.at[pl.ds(dest * mb, mb)], back_r.at[p], bs_send.at[d], bs_recv.at[p], dest, q)

    def collect_back():
        total = back_t[pl.ds(p * mb, mb)]
        for d in range(1, n_row):
            peer = (p + d) % n_row
            to(back_r.at[peer], back_r.at[peer], bs_send.at[d], bs_recv.at[peer], peer, q).wait_recv()
            total = total + back_r[peer]
        for m in range(mb):
            back[:, m, :] = total[m]

    def form_flags():
        for k in range(2):
            when(head & (core == k), own_col[1].wait)
            when(jnp.logical_not(head & (core == k)), to(fill, cflag.at[k], cf_send.at[0], cf_recv.at[k], p, sibling).wait_recv)
            when(p == k, own_row[1].wait, own_row[2].wait)
            when(p != k, *[to(small.at[k, x], small.at[k, x], sm_send.at[x, 0], sm_recv.at[k, x], p, sibling).wait_recv for x in range(2)])
            when((p == k) & jnp.logical_not(head & (core == 1 - k)), own_row[3].wait)
            when((p != k) & jnp.logical_not(head & (core == 1 - k)), to(fill, rflag.at[k], rf_send.at[0], rf_recv.at[k], p, sibling).wait_recv)
            when(jnp.logical_not(head & (core == k)), to(rflag.at[0], kflag.at[k], kf_send.at[0], kf_recv.at[k], p, sibling).wait_recv)
        corner_sib(1 - core).wait_recv()
        when(p < 2, own_row[0].wait)
        loads[2].wait()
        loads[3].wait()
        when(head, own_col[0].wait)

        @pl.when(head)
        def _():
            for k in range(2):
                rowbuf[k, 0] = jnp.zeros((width, width), F32)

        eye = (lax.broadcasted_iota(jnp.int32, (rows, rows), 0) == lax.broadcasted_iota(jnp.int32, (rows, rows), 1)).astype(F32)
        for k in range(2):
            line = cflag[k, 0:1, :].astype(F32)
            cexp[k] = jnp.broadcast_to(jnp.sum(line * eye, axis=1, keepdims=True), (rows, width))
            rexp[k] = jnp.broadcast_to(rflag[k, :, 0:1].astype(F32), (cols, width))
        for k in range(2):
            h, l = split(piv[k])
            kh[k] = h
            kl[k] = l
            h, l = split(colbuf[k, rows] * kflag[k, 0:1, 0:1].astype(F32))
            kh[2 + k] = h
            kl[2 + k] = l
        lower = mul3(kh[2], kl[2], kh[0], kl[0])
        h, l = split(lower)
        l10[0] = h
        l10[1] = l
        eh, el = split(mul3(kh[0], kl[0], kh[3], kl[3]))
        th, tl = split(-mul3(eh, el, kh[1], kl[1]))
        wh[0:width, 0:width] = kh[0]
        wl[0:width, 0:width] = kl[0]
        wh[0:width, width:] = th
        wl[0:width, width:] = tl
        wh[width:, 0:width] = jnp.zeros((width, width), BF16)
        wl[width:, 0:width] = jnp.zeros((width, width), BF16)
        wh[width:, width:] = kh[1]
        wl[width:, width:] = kl[1]
        y1 = small[1, 0] - thin(stack(small[0, 0]), h, l, NT)
        for k, y in ((0, small[0, 0]), (1, y1)):
            ytop[k] = y
            h, l = split(y)
            ypair[0:modes, k * width:(k + 1) * width] = h
            ypair[modes:, k * width:(k + 1) * width] = l
            for d in range(n_col):
                ycut[k, d] = y[d * mi:(d + 1) * mi]

    def form(g):
        for t in range(group):
            sib(g * group + t, 1 - core).wait_recv()
        blocks = []
        for t in range(group):
            a = g * group + t
            blocks.append(jnp.concatenate([colbuf[k, a] * cexp[k, a:a + 1, :] for k in range(2)], axis=1))
        n = group // 2
        lower = []
        for s in range(2):
            h, l = split(jnp.concatenate(blocks[s * n:(s + 1) * n], axis=0))
            lower.append(mul3(h, l, wh[...], wl[...]))
        lower = jnp.concatenate(lower, axis=0)
        if g == 0:
            m0 = jnp.where(p > 0, 1.0, 0.0)
            m1 = jnp.where(p > 1, 1.0, 0.0)
            l0 = lower[0:width, 0:width] * m0
            l1 = lower[0:width, width:] * m1
            xh, xl = split(l0)
            mid = blocks[0][:, width:] - mul3(xh, xl, kh[3], kl[3])
            first[:, 0:width] = jnp.where(p > 0, l0, blocks[0][:, 0:width])
            first[:, width:] = jnp.where(p > 1, l1, mid)
            lower = jnp.concatenate([jnp.concatenate([l0, l1], axis=1), lower[width:]], axis=0)
        for k in range(2):
            @pl.when(q == k)
            def _(k=k):
                for t in range(group):
                    a = g * group + t
                    if a == 0:
                        fact[a, 0] = first[:, k * width:(k + 1) * width]
                    else:
                        fact[a, 0] = lower[t * width:(t + 1) * width, k * width:(k + 1) * width]
        h, l = split(lower)
        lo, size = g * group * width, group * width
        lh[lo:lo + size, :] = h
        ll[lo:lo + size, :] = l
        for s in range(2):
            cut = s * n * width
            change = thin(ypair[...], h[cut:cut + n * width], l[cut:cut + n * width], NT)
            for t in range(n):
                a = g * group + s * n + t
                y_out[a] = drv[a] - change[:, t * width:(t + 1) * width]

    owner = q % n_row
    assert n_col == 2 * n_row and rows == 2 * cols

    def y_copy(d):
        return to(ysel, ysel, y_send.at[d], y_recv, (p + d) % n_row, q)

    def send_y():
        @pl.when(p == owner)
        def _():
            when((p != 0) | (q != 0), to(ysel, ysel, yp_send, yp_recv, p, sibling).wait_recv)
            for d in range(1, n_row):
                y_copy(d).start()

        drains.append((p == owner, [y_copy(d).wait_send for d in range(1, n_row)]))

    def t_copy():
        return to(tcut, trecv, t_send, t_recv, p, sibling)

    def yp_copy():
        return to(yown, ysel, yp_send, yp_recv, p, core * n_row + p)

    def early_y():
        wide = thin(ypair[...], wh[...], wl[...], NT)
        coef = stack(jnp.where(core == 0, wide[:, 0:width], wide[:, width:]))
        n = rows // 2
        for s in range(2):
            lo = s * n * width
            part = thin(coef, mh[lo:lo + n * width, 0:width], ml[lo:lo + n * width, 0:width], NT)
            for t in range(n):
                ximg[s * n + t] = part[:, t * width:(t + 1) * width]
        for c in range(cols):
            tcut[c] = ximg[2 * c + 1 - core]
        t_copy().start()

    def early_sum():
        t_copy().wait_recv()
        for c in range(cols):
            yown[c] = drv[2 * c + core] - ximg[2 * c + core] - trecv[c]

        @pl.when((p < 2) & (core == 0))
        def _():
            yown[0] = ytop[slot]

        when(core * n_row + p != q, yp_copy().start)

        @pl.when(core * n_row + p == q)
        def _():
            ysel[...] = yown[...]

    def only(cond, f):
        return lambda: when(cond, f)

    def early(*fs):
        def run():
            when(head, *fs)
        return run

    def take_y():
        when(p != owner, to(ysel, ysel, y_send.at[0], y_recv, p, sibling).wait_recv)
        for c in range(cols):
            keep = jnp.where(head, 0.0, 1.0) if c == 0 else 1.0
            h, l = split(ysel[c] * keep)
            yst[0:modes, c * width:(c + 1) * width] = h
            yst[modes:, c * width:(c + 1) * width] = l

    def piece_image(g):
        n = group // 2
        for s in range(2):
            lo = (g * group + s * n) * width
            part = thin(yst[...], mh[lo:lo + n * width, :], ml[lo:lo + n * width, :], NT)
            for t in range(n):
                ximg[g * group + s * n + t] = part[:, t * width:(t + 1) * width]

    def x_copy(d):
        dest = (q + d) % n_col
        return to(x0t.at[dest], x0r.at[q], x_send.at[d], x_recv.at[q], p, dest)

    def send_x0():
        @pl.when(p < 2)
        def _():
            for d in range(n_col):
                x0t[d] = ximg[0, d * mi:(d + 1) * mi, :]
            for d in range(1, n_col):
                x_copy(d).start()

        drains.append((p < 2, [x_copy(d).wait_send for d in range(1, n_col)]))

    def v_copy(d):
        return to(vloc, vbuf.at[slot], v_send.at[d], v_recv.at[slot], (p + d) % n_row, q)

    def send_v():
        @pl.when(p < 2)
        def _():
            total = x0t[q]
            for d in range(1, n_col):
                peer = (q + d) % n_col
                to(x0r.at[peer], x0r.at[peer], x_send.at[d], x_recv.at[peer], p, peer).wait_recv()
                total = total + x0r[peer]
            vloc[...] = total
            vbuf[slot] = total
            for d in range(1, n_row):
                v_copy(d).start()

        drains.append((p < 2, [v_copy(d).wait_send for d in range(1, n_row)]))

    def img_copy(d):
        dest = (q + d) % n_col
        return to(img_t.at[pl.ds(dest * mi, mi)], img_r.at[q], is_send.at[d], is_recv.at[q], p, dest)

    def send_image():
        for m in range(modes):
            img_t[m] = ximg[:, m, :]
        for d in range(1, n_col):
            img_copy(d).start()
        drains.append((None, [img_copy(d).wait_send for d in range(1, n_col)]))

    def collect_image():
        for k in range(2):
            when(p != k, to(vbuf.at[k], vbuf.at[k], v_send.at[0], v_recv.at[k], p, sibling).wait_recv)
        x0 = vbuf[0]
        pad = jnp.zeros((8 - mi, width), F32)
        v1 = vbuf[1] - thin(stack(jnp.concatenate([x0, pad], axis=0)), l10[0], l10[1], NT)[0:mi]
        y0, y1 = ycut[0, q], ycut[1, q]
        wide = jnp.zeros((8 - mi, 2 * width), F32)

        def padded(g0, g1):
            return stack(jnp.concatenate([jnp.concatenate([g0, g1], axis=1), wide], axis=0))

        pair = padded(y0 - x0, y1 - v1)
        n = rows * width // 2
        fix = jnp.concatenate([thin(pair, lh[x:x + n, :], ll[x:x + n, :], NT) for x in (0, n)], axis=1)
        g0 = y0 - jnp.where(p > 0, x0, 0.0)
        g1 = y1 - jnp.where(p > 1, v1, 0.0)
        fh, fl = split(first[...])
        head_fix = thin(padded(g0, g1), fh, fl, NT)
        total = img_t[pl.ds(q * mi, mi)]
        for d in range(1, n_col):
            peer = (q + d) % n_col
            to(img_r.at[peer], img_r.at[peer], is_send.at[d], is_recv.at[peer], p, peer).wait_recv()
            total = total + img_r[peer]
        for a in range(rows):
            change = head_fix if a == 0 else fix[:, a * width:(a + 1) * width]
            image[a] = (total[:, a, :] + change[0:mi]) * scale

    def update(c):
        row_arrive(c)
        row_arrive(c + 1)
        u0 = jnp.concatenate([rowbuf[0, x] * rexp[0, x:x + 1, :] for x in (c, c + 1)], axis=1)
        u1 = jnp.concatenate([rowbuf[1, x] * rexp[1, x:x + 1, :] for x in (c, c + 1)], axis=1)
        h0, l0 = split(u0)
        h1, l1 = split(u1 - mul3(l10[0], l10[1], h0, l0))
        uh[0:width, :] = h0
        ul[0:width, :] = l0
        uh[width:, :] = h1
        ul[width:, :] = l1
        n = rows // 2
        for s in range(2):
            lo = s * n * width
            change = mul3(lh[lo:lo + n * width, :], ll[lo:lo + n * width, :], uh[...], ul[...])
            for t in range(n):
                a = s * n + t
                for e in range(2):
                    value = fact[a, c + e] * flags[c + e, a].astype(F32)
                    value = value - change[t * width:(t + 1) * width, e * width:(e + 1) * width]
                    if c + e == 0:
                        value = jnp.where(head, fact[a, 0], value)
                    fact[a, c + e] = value

    ring_end = half - 1 + 2 * (chips - 1)
    row_end = 2 * cols + lag
    steps = []
    done = [0]

    def tick(k):
        def ring_tick():
            ring_step(k)
            corner_step(k)
        steps.append(ring_tick)
        pass_row()

    def pass_row(count=1):
        for _ in range(count):
            if done[0] < row_end:
                steps.append(functools.partial(row_step, done[0]))
                done[0] += 1

    def work(f, *args):
        steps.append(functools.partial(f, *args))

    first_form = corner_end
    late = max(ring_end, corner_end) + 1
    for k in range(late - 1):
        tick(k)
        if k in (4, 8, 11):
            pass_row()
        if k == 0:
            work(start_flags)
        if k < 4:
            work(piece_back, k)
        if k == 3:
            work(send_s)
        if k == met + 1:
            work(early(form_flags, early_y))
        if k == met + 2:
            work(early(early_sum))
        if k == met + 3:
            work(only(p > 1, finish_back))
        if k == met + 5:
            work(send_y)
        if k == met + 6:
            work(gather_s)
    drains.append((head, [t_copy().wait_send]))
    drains.append((head & (core * n_row + p != q), [yp_copy().wait_send]))
    work(take_y)
    work(piece_image, 0)
    work(send_x0)
    pass_row()
    work(only(jnp.logical_not(head), form_flags))
    work(solve_z)
    work(form, 0)
    work(form, 1)
    tick(late - 1)
    work(form, 2)
    for g in range(1, 4):
        pass_row()
        work(piece_image, g)
    work(send_image)
    pass_row()
    work(only(p < 2, finish_back))
    drains.append((None, [back_copy(d).wait_send for d in range(1, n_row)]))
    pass_row()
    work(form, 3)
    pass_row()
    work(update, 0)
    pass_row(row_end)
    for c in range(2, cols - 2, 2):
        work(update, c)
        if c == 2:
            work(send_v)
    work(only(p == last, collect_image))
    work(update, cols - 2)
    work(collect_back)
    work(only(p != last, collect_image))
    for step in steps:
        step()

    for cond, fs in drains:
        if cond is None:
            for f in fs:
                f()
        else:
            when(cond, *fs)
    for block in range(rows):
        stop = chips - 1 if block % 2 == 0 else 1
        due = (pos != 0) & (pos != stop)
        if block >= rows - 2 * depth:
            due = due | (pos == 0)
        when(due, ring(block, after).wait_send)
        sib(block, core).wait_send()
    for c in range(cols):
        when((p == 1) & present(c), row_copy(1, c, False).wait_send)
        when((p == 0) & present(c), row_copy(0, c, True).wait_send)
        if n_row > 2:
            when((p == 1) & present(c), row_copy(0, c, True).wait_send, row_copy(1, c, True).wait_send)
        if n_row > 3:
            for k in range(2):
                when((p >= 2) & (p < last) & present(c), row_copy(k, c, True).wait_send)


def store_kernel(fact, y, z, img, bck, out, y_out, z_out, img_out, bck_out, sems):
    parts = 8
    n = fact.shape[0] // parts
    copies = [
        pltpu.make_async_copy(fact.at[pl.ds(i * n, n)], out.at[pl.ds(i * n, n)], sems.at[i]) for i in range(parts)
    ]
    for i, (src, dst) in enumerate(((y, y_out), (z, z_out), (img, img_out), (bck, bck_out))):
        copies.append(pltpu.make_async_copy(src, dst, sems.at[parts + i]))
    for copy in copies:
        copy.start()
    for copy in copies:
        copy.wait()


def shards(trace, fill, pivots, direct_rhs, adjoint_rhs):
    n_row, n_col = lax.axis_size("row"), lax.axis_size("col")
    rows, cols, width = trace.shape[0], trace.shape[2], trace.shape[4]
    modes = direct_rhs.shape[2]
    blocks = trace.reshape(rows, cols, width, width)
    flags = fill.reshape(rows, cols).T
    mi, mb = modes // n_col, modes // n_row
    hbm = pl.BlockSpec(memory_space=pltpu.HBM)
    vmem = pl.BlockSpec(memory_space=pltpu.VMEM)
    shape = jax.ShapeDtypeStruct
    dma = pltpu.SemaphoreType.DMA
    V = pltpu.VMEM
    outs = pl.pallas_call(
        functools.partial(comm_kernel, n_row, n_col),
        out_shape=(
            shape((rows, cols, width, width), F32),
            shape((rows, modes, width), F32),
            shape((rows, modes, width), F32),
            shape((rows, mi, width), F32),
            shape((cols, mb, width), F32),
        ),
        in_specs=[hbm] * 5,
        out_specs=[vmem] * 5,
        scratch_shapes=[
            V((2, rows + 1, width, width), F32),
            V((2, cols, width, width), F32),
            V((2, 2, modes, width), F32),
            V((rows, modes, width), F32),
            V((rows, modes, width), F32),
            V((2, width, width), F32),
            pltpu.SMEM((cols, rows), jnp.int32),
            V((2, cols, rows), jnp.int32),
            V((2, cols, rows), jnp.int32),
            V((2, cols, rows), jnp.int32),
            V((2, rows, width), F32),
            V((2, cols, width), F32),
            V((rows * width, cols * width), BF16),
            V((rows * width, cols * width), BF16),
            V((rows * width, 2 * width), BF16),
            V((rows * width, 2 * width), BF16),
            V((2 * width, 2 * width), BF16),
            V((2 * width, 2 * width), BF16),
            V((4, width, width), BF16),
            V((4, width, width), BF16),
            V((2, width, width), BF16),
            V((2 * width, 2 * width), BF16),
            V((2 * width, 2 * width), BF16),
            V((width, 2 * width), F32),
            V((2 * modes, rows * width), BF16),
            V((2 * modes, cols * width), BF16),
            V((2 * modes, 2 * width), BF16),
            V((2, modes, width), F32),
            V((cols, modes, width), F32),
            V((cols, modes, width), F32),
            V((cols, modes, width), F32),
            V((cols, modes, width), F32),
            V((2, n_col, mi, width), F32),
            V((modes, cols * width), F32),
            V((modes, width), F32),
            V((n_row, modes, width), F32),
            V((modes, width), F32),
            V((modes, width), F32),
            V((3, modes, width), F32),
            V((rows, modes, width), F32),
            V((n_col, mi, width), F32),
            V((n_col, mi, width), F32),
            V((mi, width), F32),
            V((2, mi, width), F32),
            V((modes, rows, width), F32),
            V((n_col, mi, rows, width), F32),
            V((modes, cols, width), F32),
            V((n_row, mb, cols, width), F32),
            dma((4,)), dma((11,)),
            dma((n_col,)), dma((2,)), dma((n_row,)), dma((2,)), dma((2, n_row)), dma((2, 2)),
            dma((n_row,)), dma, dma((n_col,)), dma((2,)), dma((3,)), dma((2,)),
            dma((rows,)), dma((rows,)), dma((rows,)), dma((rows,)),
            dma((2, cols)), dma((2, cols)), dma((2, cols)),
            dma((2,)), dma((n_row,)), dma, dma, dma((n_col,)), dma, dma((n_row,)), dma, dma, dma, dma, dma,
            dma((n_col,)), dma((n_col,)), dma((n_row,)), dma((2,)),
            dma((n_col,)), dma((n_col,)), dma((n_row,)), dma((n_row,)),
        ],
        compiler_params=pltpu.CompilerParams(
            collective_id=0, has_side_effects=True, vmem_limit_bytes=40 * 1024 * 1024
        ),
    )(*[pltpu.with_memory_space_constraint(x, pltpu.HBM) for x in (blocks, flags, pivots, direct_rhs[:, 0], adjoint_rhs[:, 0])])
    factored, direct, adjoint, image, back = pl.pallas_call(
        store_kernel,
        out_shape=tuple(shape(x.shape, F32) for x in outs),
        in_specs=[vmem] * 5,
        out_specs=[hbm] * 5,
        scratch_shapes=[dma((12,))],
        compiler_params=pltpu.CompilerParams(vmem_limit_bytes=16 * 1024 * 1024),
    )(*outs)
    return (
        factored[:, None, :, None],
        direct[:, None],
        adjoint[:, None],
        image[:, None],
        back[:, None],
    )


def solution(mesh):
    placed = (
        P(None, "row", None, "col", None, None),
        P(None, "row", None, "col"),
        P(),
        P(None, "row", None, None),
        P(None, "row", None, None),
    )
    return jax.shard_map(
        shards,
        mesh=mesh,
        in_specs=placed,
        out_specs=(
            P(None, "row", None, "col", None, None),
            P(None, "row", None, None),
            P(None, "row", None, None),
            P(None, "row", "col", None),
            P(None, "col", "row", None),
        ),
        check_vma=False,
    )
```

```python
import functools

import jax
import jax.numpy as jnp
from jax import lax
from jax.experimental import pallas as pl
from jax.experimental.pallas import tpu as pltpu
from jax.sharding import PartitionSpec as P

F32 = jnp.float32
BF16 = jnp.bfloat16
NN = (((1,), (0,)), ((), ()))
NT = (((1,), (1,)), ((), ()))
MESH = pl.DeviceIdType.MESH


def split(x):
    high = x.astype(BF16)
    return high, (x - high.astype(F32)).astype(BF16)


def mul(a, b, dims=NN):
    return lax.dot_general(a, b, dims, preferred_element_type=F32)


def mul3(ah, al, bh, bl, dims=NN):
    return mul(ah, bh, dims) + mul(ah, bl, dims) + mul(al, bh, dims)


def stack(x):
    high, low = split(x)
    return jnp.concatenate([high, low], axis=0)


def thin(pair, bh, bl, dims=NN):
    half = pair.shape[0] // 2
    both = mul(pair, bh, dims)
    return both[:half] + both[half:] + mul(pair[:half], bl, dims)


def comm_kernel(
    n_row, n_col, trace, fill, pivots, direct, adjoint,
    done_fact, y_out, z_out, image, back,
    fact, colbuf, rowbuf, small, drv, arv, piv, flags, cflag, rflag, kflag, cexp, rexp,
    mh, ml, lh, ll, wh, wl, kh, kl, l10, uh, ul, first, zst, yst, ypair, ytop, ysel, yown, tcut, trecv, ycut,
    backp, sloc, sbuf, stot, ssib, zmsg, ximg, x0t, x0r, vloc, vbuf,
    img_t, img_r, back_t, back_r,
    store, load, local, cf_send, cf_recv, rf_send, rf_recv, sm_send, sm_recv,
    kz_send, kz_recv, kf_send, kf_recv, corner_send, corner_recv,
    ring_send, ring_recv, sib_send, sib_recv, row_up, row_down, row_recv,
    s_send, s_recv, ss_send, ss_recv, z_send, z_recv, y_send, y_recv, t_send, t_recv, yp_send, yp_recv,
    x_send, x_recv, v_send, v_recv, is_send, is_recv, bs_send, bs_recv,
):
    rows, cols, width = fact.shape[0], fact.shape[1], fact.shape[2]
    modes = y_out.shape[1]
    mi, mb = modes // n_col, modes // n_row
    scale = (rows * n_row * width) ** (-0.5)
    p = lax.axis_index("row")
    q = lax.axis_index("col")
    chips = n_col // 2
    deep = chips // 2
    chip, core = q // 2, q % 2
    cy, cx = chip // 2, chip % 2
    pos = cx * (cy + 1) + (1 - cx) * ((chips - cy) % chips)
    half = rows // 2
    group = rows // 4
    last = n_row - 1
    head = q < 2
    pf = p.astype(F32)

    def at_pos(r):
        side = 1 - ((r + chips - 1) % chips) // deep
        return (side * ((r - 1) * 2 + 1) + (1 - side) * (((chips - r) % chips) * 2)) * 2 + core

    after = at_pos((pos + 1) % chips)
    before = at_pos((pos + chips - 1) % chips)
    sibling = chip * 2 + 1 - core
    up = (p + 1) % n_row
    down = (p + n_row - 1) % n_row
    drains = []
    depth = 3
    met = 4

    def to(src, dst, send, recv, row, col):
        return pltpu.make_async_remote_copy(
            src_ref=src, dst_ref=dst, send_sem=send, recv_sem=recv,
            device_id=(row, col), device_id_type=MESH,
        )

    def send(copy):
        copy.start()

    def when(cond, *fs):
        @pl.when(cond)
        def _():
            for f in fs:
                f()

    barrier = pltpu.get_barrier_semaphore()
    for d in range(1, n_col):
        pl.semaphore_signal(barrier, inc=1, device_id=(p, (q + d) % n_col), device_id_type=MESH)
    for d in range(1, n_row):
        pl.semaphore_signal(barrier, inc=1, device_id=((p + d) % n_row, q), device_id_type=MESH)

    loads = [
        pltpu.make_async_copy(fill, flags, local.at[0]),
        pltpu.make_async_copy(adjoint, arv, local.at[1]),
        pltpu.make_async_copy(direct, drv, local.at[2]),
        pltpu.make_async_copy(pivots, piv, local.at[3]),
    ]
    for x in loads:
        x.start()
    bulk = [
        pltpu.make_async_copy(trace.at[pl.ds(g * group, group)], fact.at[pl.ds(g * group, group)], load.at[g])
        for g in range(4)
    ]
    for x in bulk:
        x.start()
    slot = lax.rem(p, 2)
    own_row = [
        pltpu.make_async_copy(trace.at[0], rowbuf.at[slot], local.at[4]),
        pltpu.make_async_copy(direct.at[0], small.at[slot, 0], local.at[5]),
        pltpu.make_async_copy(adjoint.at[0], small.at[slot, 1], local.at[6]),
        pltpu.make_async_copy(fill, rflag.at[slot], local.at[7]),
    ]
    own_col = [
        pltpu.make_async_copy(trace.at[:, 0], colbuf.at[core, pl.ds(0, rows)], local.at[8]),
        pltpu.make_async_copy(fill, cflag.at[core], local.at[9]),
    ]
    own_corner = pltpu.make_async_copy(trace.at[0, 0], colbuf.at[core, rows], local.at[10])
    when(p < 2, *[x.start for x in own_row])
    when(head, *[x.start for x in own_col])
    when(head & (p == 1 - core), own_corner.start)

    pl.semaphore_wait(barrier, n_col + n_row - 2)

    def cf_copy(d):
        return to(fill, cflag.at[core], cf_send.at[d], cf_recv.at[core], p, (q + d) % n_col)

    def rf_copy(d):
        return to(fill, rflag.at[slot], rf_send.at[d], rf_recv.at[slot], (p + d) % n_row, q)

    def sm_copy(kind, d):
        src = (direct, adjoint)[kind].at[0]
        return to(src, small.at[slot, kind], sm_send.at[kind, d], sm_recv.at[slot, kind], (p + d) % n_row, q)

    def kz_copy(d):
        return to(trace.at[0, 0], colbuf.at[core, rows], kz_send.at[d], kz_recv, (p + d) % n_row, q)

    when(head & (p == 1 - core), *[kz_copy(d).start for d in range(1, n_row)])
    drains.append((head & (p == 1 - core), [kz_copy(d).wait_send for d in range(1, n_row)]))
    smalls = [rf_copy(d) for d in range(1, n_row)]
    smalls += [sm_copy(kind, d) for d in range(1, n_row) for kind in range(2)]
    when(p < 2, *[x.start for x in smalls])
    drains.append((p < 2, [x.wait_send for x in smalls]))
    plane = [cf_copy(d) for d in range(1, n_col)]
    when(head, *[x.start for x in plane])
    drains.append((head, [x.wait_send for x in plane]))

    def ring(block, dest):
        ref = colbuf.at[core, block]
        index = jnp.where(head, block, lax.rem(block, 2))
        return to(ref, ref, ring_send.at[index], ring_recv.at[block], p, dest)

    def ring_first(block, dest):
        return to(trace.at[block, 0], colbuf.at[core, block], ring_send.at[block], ring_recv.at[block], p, dest)

    def sib(block, which):
        ref = colbuf.at[which, block]
        return to(ref, ref, sib_send.at[0], sib_recv.at[block], p, sibling)

    def sib_first(block):
        return to(trace.at[block, 0], colbuf.at[core, block], sib_send.at[0], sib_recv.at[block], p, sibling)

    def ring_step(k):
        for j in range(min(depth, half)) if k == 0 else range(max(k, depth), min(k + 1, half)):
            if j >= depth:
                when(head, ring(2 * (j - depth), after).wait_send, ring(2 * (j - depth) + 1, before).wait_send)
            when(
                head, ring_first(2 * j, after).start, ring_first(2 * j + 1, before).start,
                sib_first(2 * j).start, sib_first(2 * j + 1).start,
            )
        for forward in (True, False):
            s = k - 2 * (pos if forward else chips - pos)
            block = 2 * s + (0 if forward else 1)
            dest = after if forward else before
            stop = chips - 1 if forward else 1

            @pl.when((pos != 0) & (s >= 0) & (s < half))
            def _(block=block, dest=dest, stop=stop):
                ring(block, dest).wait_recv()
                when(pos != stop, ring(block, dest).start)
                sib(block, core).start()

    def row_copy(k, c, upward, own=False):
        src = trace.at[0, c] if own else rowbuf.at[k, c]
        sems = row_up if upward else row_down
        return to(src, rowbuf.at[k, c], sems.at[k, 0], row_recv.at[k, c], up if upward else down, q)

    lag = 8 + 2 * (n_row - 4) if n_row > 3 else 0

    def present(c):
        return (q >= 2) if c == 0 else (q >= 0)

    def row_step(k):
        if k == 0:
            for c in range(cols):
                when((p == 0) & present(c), row_copy(0, c, True, True).start)
                if n_row > 2:
                    when((p == 1) & present(c), row_copy(1, c, True, True).start)
                when((p == 1) & present(c), row_copy(1, c, False, True).start)
        if n_row > 2 and cols <= k < 2 * cols:
            c = k - cols
            when((p == 1) & present(c), row_copy(0, c, True).wait_recv, row_copy(0, c, True).start)
        if n_row > 3:
            i = k - 4 - 2 * (p - 2) - jnp.where(head, 4, 0)
            kk = jnp.where(i < cols, 1, 0)
            c = lax.rem(i, cols)

            @pl.when((p >= 2) & (p < last) & (i >= 0) & (i < 2 * cols) & ((c > 0) | (q >= 2)))
            def _():
                copy = row_copy(kk, c, True)
                copy.wait_recv()
                copy.start()

    def row_arrive(c):
        for k in range(2):
            passes = (p > k) & (p + 1 < n_row)
            when((p != k) & jnp.logical_not(passes) & present(c), row_copy(k, c, True).wait_recv)

    def corner(forward, dest):
        ref = colbuf.at[core, rows]
        return to(ref, ref, corner_send.at[0 if forward else 1], corner_recv.at[0], p, dest)

    def corner_sib(which):
        ref = colbuf.at[which, rows]
        return to(ref, ref, corner_send.at[2], corner_recv.at[1], p, sibling)

    def kf_copy(d):
        return to(rflag.at[1 - core], kflag.at[core], kf_send.at[d], kf_recv.at[core], p, (q + d) % n_col)

    def corner_step(k):
        if k == met:
            when(head & (p == 1 - core), own_corner.wait, own_row[3].wait)
            when(head & (p != 1 - core), kz_copy(0).wait_recv, to(fill, rflag.at[1 - core], rf_send.at[0], rf_recv.at[1 - core], p, sibling).wait_recv)
            when(
                head, corner(True, after).start, corner(False, before).start, corner_sib(core).start,
                *[kf_copy(d).start for d in range(1, n_col)],
            )
            drains.append((head, [corner(True, after).wait_send, corner(False, before).wait_send, corner_sib(core).wait_send]))
            drains.append((head, [kf_copy(d).wait_send for d in range(1, n_col)]))

            @pl.when(head)
            def _():
                kflag[core] = rflag[1 - core]

        if k > met + 1 and (k - met - 1) % 3 == 0:
            hop = (k - met - 1) // 3
            if hop <= deep:
                @pl.when(pos == hop)
                def _():
                    corner(True, after).wait_recv()
                    if hop < deep:
                        corner(True, after).start()
                    corner_sib(core).start()

                if hop < deep:
                    drains.append((pos == hop, [corner(True, after).wait_send]))
                drains.append((pos == hop, [corner_sib(core).wait_send]))
            other = chips - hop
            if other > deep:
                @pl.when(pos == other)
                def _():
                    corner(False, before).wait_recv()
                    if other > deep + 1:
                        corner(False, before).start()
                    corner_sib(core).start()

                if other > deep + 1:
                    drains.append((pos == other, [corner(False, before).wait_send]))
                drains.append((pos == other, [corner_sib(core).wait_send]))

    corner_end = met + 1 + 3 * max(deep, chips - deep - 1)

    def start_flags():
        loads[0].wait()
        loads[1].wait()
        for a in range(rows):
            keep = jnp.where(p < 2, 0.0, 1.0) if a == 0 else 1.0
            h, l = split(arv[a] * keep)
            zst[0:modes, a * width:(a + 1) * width] = h
            zst[modes:2 * modes, a * width:(a + 1) * width] = l
        z_out[...] = arv[...]

    def piece_back(g):
        bulk[g].wait()
        for t in range(group):
            a = g * group + t
            for c in range(cols):
                h, l = split(fact[a, c] * flags[c, a].astype(F32))
                mh[a * width:(a + 1) * width, c * width:(c + 1) * width] = h
                ml[a * width:(a + 1) * width, c * width:(c + 1) * width] = l
        lo, n = g * group * width, group * width
        part = thin(zst[:, lo:lo + n], mh[lo:lo + n, :], ml[lo:lo + n, :])
        if g == 0:
            backp[...] = part
        else:
            backp[...] += part

    def s_copy(dest):
        return to(sloc, sbuf.at[p], s_send.at[dest], s_recv.at[p], dest, q)

    def send_s():
        @pl.when(head)
        def _():
            sloc[...] = backp[:, 0:width]
            for dest in range(2):
                when(p != dest, s_copy(dest).start)
            backp[:, 0:width] = jnp.zeros((modes, width), F32)

        for dest in range(2):
            drains.append((head & (p != dest), [s_copy(dest).wait_send]))

    def ss_copy():
        return to(stot, ssib, ss_send, ss_recv, p, sibling)

    def gather_s():
        @pl.when(head & (p < 2))
        def _():
            total = sloc[...]
            for r in range(n_row):
                when(p != r, to(sloc, sbuf.at[r], s_send.at[0], s_recv.at[r], p, sibling).wait_recv)
                total = total + jnp.where(p == r, 0.0, sbuf[r])
            stot[...] = total
            when(core == 1, ss_copy().start)

        drains.append((head & (p < 2) & (core == 1), [ss_copy().wait_send]))

    def z_copy(d):
        return to(zmsg, zmsg, z_send.at[d], z_recv, p, (q + d) % n_col)

    def solve_z():
        @pl.when((q == 0) & (p < 2))
        def _():
            ss_copy().wait_recv()
            w0 = thin(stack(stot[...]), kh[0], kl[0])
            w1 = thin(stack(ssib[...] - thin(stack(w0), kh[3], kl[3])), kh[1], kl[1])
            z1 = small[1, 1] - w1
            z1l = thin(stack(thin(stack(z1), kh[2], kl[2])), kh[0], kl[0])
            z0 = small[0, 1] - w0 - z1l
            a1 = z1 - w1
            a0 = z0 - w0 - thin(stack(thin(stack(a1), kh[2], kl[2])), kh[0], kl[0])
            zmsg[0] = jnp.where(p == 0, z0, z1)
            zmsg[1] = jnp.where(p == 0, a0, a1)
            zmsg[2] = z0 - z1l
            for d in range(1, n_col):
                z_copy(d).start()

        drains.append(((q == 0) & (p < 2), [z_copy(d).wait_send for d in range(1, n_col)]))

    def finish_back():
        @pl.when(p < 2)
        def _():
            when(q != 0, z_copy(0).wait_recv)
            z_out[0] = zmsg[0]
            a = zmsg[1]
            b = jnp.where(q == 0, jnp.where(p == 0, zmsg[0], 0.0), jnp.where(p == 0, zmsg[2], zmsg[0]))
            b = jnp.where(head, b, a)
            extra = jnp.where(p == q, small[slot, 1] - zmsg[0], 0.0)
            backp[:, 0:width] += thin(stack(b), mh[0:width, 0:width], ml[0:width, 0:width]) + extra
            backp[:, width:] += thin(stack(a), mh[0:width, width:], ml[0:width, width:])

        for c in range(cols):
            for m in range(modes):
                pass
        for c in range(cols):
            ximg[c] = backp[:, c * width:(c + 1) * width] * scale
        for m in range(modes):
            back_t[m] = ximg[0:cols, m, :]
        for d in range(1, n_row):
            back_copy(d).start()

    def back_copy(d):
        dest = (p + d) % n_row
        return to(back_t.at[pl.ds(dest * mb, mb)], back_r.at[p], bs_send.at[0], bs_recv.at[p], dest, q)

    def collect_back():
        total = back_t[pl.ds(p * mb, mb)]
        for d in range(1, n_row):
            peer = (p + d) % n_row
            to(back_r.at[peer], back_r.at[peer], bs_send.at[d], bs_recv.at[peer], peer, q).wait_recv()
            total = total + back_r[peer]
        for m in range(mb):
            back[:, m, :] = total[m]

    def form_flags():
        for k in range(2):
            when(head & (core == k), own_col[1].wait)
            when(jnp.logical_not(head & (core == k)), to(fill, cflag.at[k], cf_send.at[0], cf_recv.at[k], p, sibling).wait_recv)
            when(p == k, own_row[1].wait, own_row[2].wait)
            when(p != k, *[to(small.at[k, x], small.at[k, x], sm_send.at[x, 0], sm_recv.at[k, x], p, sibling).wait_recv for x in range(2)])
            when((p == k) & jnp.logical_not(head & (core == 1 - k)), own_row[3].wait)
            when((p != k) & jnp.logical_not(head & (core == 1 - k)), to(fill, rflag.at[k], rf_send.at[0], rf_recv.at[k], p, sibling).wait_recv)
            when(jnp.logical_not(head & (core == k)), to(rflag.at[0], kflag.at[k], kf_send.at[0], kf_recv.at[k], p, sibling).wait_recv)
        corner_sib(1 - core).wait_recv()
        when(p < 2, own_row[0].wait)
        loads[2].wait()
        loads[3].wait()
        when(head, own_col[0].wait)

        @pl.when(head)
        def _():
            for k in range(2):
                rowbuf[k, 0] = jnp.zeros((width, width), F32)

        eye = (lax.broadcasted_iota(jnp.int32, (rows, rows), 0) == lax.broadcasted_iota(jnp.int32, (rows, rows), 1)).astype(F32)
        for k in range(2):
            line = cflag[k, 0:1, :].astype(F32)
            cexp[k] = jnp.broadcast_to(jnp.sum(line * eye, axis=1, keepdims=True), (rows, width))
            rexp[k] = jnp.broadcast_to(rflag[k, :, 0:1].astype(F32), (cols, width))
        for k in range(2):
            h, l = split(piv[k])
            kh[k] = h
            kl[k] = l
            h, l = split(colbuf[k, rows] * kflag[k, 0:1, 0:1].astype(F32))
            kh[2 + k] = h
            kl[2 + k] = l
        lower = mul3(kh[2], kl[2], kh[0], kl[0])
        h, l = split(lower)
        l10[0] = h
        l10[1] = l
        eh, el = split(mul3(kh[0], kl[0], kh[3], kl[3]))
        th, tl = split(-mul3(eh, el, kh[1], kl[1]))
        wh[0:width, 0:width] = kh[0]
        wl[0:width, 0:width] = kl[0]
        wh[0:width, width:] = th
        wl[0:width, width:] = tl
        wh[width:, 0:width] = jnp.zeros((width, width), BF16)
        wl[width:, 0:width] = jnp.zeros((width, width), BF16)
        wh[width:, width:] = kh[1]
        wl[width:, width:] = kl[1]
        y1 = small[1, 0] - thin(stack(small[0, 0]), h, l, NT)
        for k, y in ((0, small[0, 0]), (1, y1)):
            ytop[k] = y
            h, l = split(y)
            ypair[0:modes, k * width:(k + 1) * width] = h
            ypair[modes:, k * width:(k + 1) * width] = l
            for d in range(n_col):
                ycut[k, d] = y[d * mi:(d + 1) * mi]

    def form(g):
        for t in range(group):
            sib(g * group + t, 1 - core).wait_recv()
        blocks = []
        for t in range(group):
            a = g * group + t
            blocks.append(jnp.concatenate([colbuf[k, a] * cexp[k, a:a + 1, :] for k in range(2)], axis=1))
        n = group // 2
        lower = []
        for s in range(2):
            h, l = split(jnp.concatenate(blocks[s * n:(s + 1) * n], axis=0))
            lower.append(mul3(h, l, wh[...], wl[...]))
        lower = jnp.concatenate(lower, axis=0)
        if g == 0:
            m0 = jnp.where(p > 0, 1.0, 0.0)
            m1 = jnp.where(p > 1, 1.0, 0.0)
            l0 = lower[0:width, 0:width] * m0
            l1 = lower[0:width, width:] * m1
            xh, xl = split(l0)
            mid = blocks[0][:, width:] - mul3(xh, xl, kh[3], kl[3])
            first[:, 0:width] = jnp.where(p > 0, l0, blocks[0][:, 0:width])
            first[:, width:] = jnp.where(p > 1, l1, mid)
            lower = jnp.concatenate([jnp.concatenate([l0, l1], axis=1), lower[width:]], axis=0)
        for k in range(2):
            @pl.when(q == k)
            def _(k=k):
                for t in range(group):
                    a = g * group + t
                    if a == 0:
                        fact[a, 0] = first[:, k * width:(k + 1) * width]
                    else:
                        fact[a, 0] = lower[t * width:(t + 1) * width, k * width:(k + 1) * width]
        h, l = split(lower)
        lo, size = g * group * width, group * width
        lh[lo:lo + size, :] = h
        ll[lo:lo + size, :] = l
        for s in range(2):
            cut = s * n * width
            change = thin(ypair[...], h[cut:cut + n * width], l[cut:cut + n * width], NT)
            for t in range(n):
                a = g * group + s * n + t
                y_out[a] = drv[a] - change[:, t * width:(t + 1) * width]

    owner = q % n_row
    assert n_col == 2 * n_row and rows == 2 * cols

    def y_copy(d):
        return to(ysel, ysel, y_send.at[d], y_recv, (p + d) % n_row, q)

    def send_y():
        @pl.when(p == owner)
        def _():
            when((p != 0) | (q != 0), to(ysel, ysel, yp_send, yp_recv, p, sibling).wait_recv)
            for d in range(1, n_row):
                y_copy(d).start()

        drains.append((p == owner, [y_copy(d).wait_send for d in range(1, n_row)]))

    def t_copy():
        return to(tcut, trecv, t_send, t_recv, p, sibling)

    def yp_copy():
        return to(yown, ysel, yp_send, yp_recv, p, core * n_row + p)

    def early_y():
        wide = thin(ypair[...], wh[...], wl[...], NT)
        coef = stack(jnp.where(core == 0, wide[:, 0:width], wide[:, width:]))
        n = rows // 2
        for s in range(2):
            lo = s * n * width
            part = thin(coef, mh[lo:lo + n * width, 0:width], ml[lo:lo + n * width, 0:width], NT)
            for t in range(n):
                ximg[s * n + t] = part[:, t * width:(t + 1) * width]
        for c in range(cols):
            tcut[c] = ximg[2 * c + 1 - core]
        t_copy().start()

    def early_sum():
        t_copy().wait_recv()
        for c in range(cols):
            yown[c] = drv[2 * c + core] - ximg[2 * c + core] - trecv[c]

        @pl.when((p < 2) & (core == 0))
        def _():
            yown[0] = ytop[slot]

        when(core * n_row + p != q, yp_copy().start)

        @pl.when(core * n_row + p == q)
        def _():
            ysel[...] = yown[...]

    def only(cond, f):
        return lambda: when(cond, f)

    def early(*fs):
        def run():
            when(head, *fs)
        return run

    def take_y():
        when(p != owner, to(ysel, ysel, y_send.at[0], y_recv, p, sibling).wait_recv)
        for c in range(cols):
            keep = jnp.where(head, 0.0, 1.0) if c == 0 else 1.0
            h, l = split(ysel[c] * keep)
            yst[0:modes, c * width:(c + 1) * width] = h
            yst[modes:, c * width:(c + 1) * width] = l

    def piece_image(g):
        n = group // 2
        for s in range(2):
            lo = (g * group + s * n) * width
            part = thin(yst[...], mh[lo:lo + n * width, :], ml[lo:lo + n * width, :], NT)
            for t in range(n):
                ximg[g * group + s * n + t] = part[:, t * width:(t + 1) * width]

    def x_copy(d):
        dest = (q + d) % n_col
        return to(x0t.at[dest], x0r.at[q], x_send.at[0], x_recv.at[q], p, dest)

    def send_x0():
        @pl.when(p < 2)
        def _():
            for d in range(n_col):
                x0t[d] = ximg[0, d * mi:(d + 1) * mi, :]
            for d in range(1, n_col):
                x_copy(d).start()

        sent = x0t.at[pl.ds(0, n_col - 1)]
        drains.append((p < 2, [to(sent, sent, x_send.at[0], x_recv.at[0], p, sibling).wait_send]))

    def v_copy(d):
        return to(vloc, vbuf.at[slot], v_send.at[0], v_recv.at[slot], (p + d) % n_row, q)

    def send_v():
        @pl.when(p < 2)
        def _():
            total = x0t[q]
            for d in range(1, n_col):
                peer = (q + d) % n_col
                to(x0r.at[peer], x0r.at[peer], x_send.at[d], x_recv.at[peer], p, peer).wait_recv()
                total = total + x0r[peer]
            vloc[...] = total
            vbuf[slot] = total
            for d in range(1, n_row):
                v_copy(d).start()

        sent = x0t.at[pl.ds(0, n_row - 1)]
        drains.append((p < 2, [to(sent, sent, v_send.at[0], v_recv.at[0], p, sibling).wait_send]))

    def img_copy(d):
        dest = (q + d) % n_col
        return to(img_t.at[pl.ds(dest * mi, mi)], img_r.at[q], is_send.at[0], is_recv.at[q], p, dest)

    def send_image():
        for m in range(modes):
            img_t[m] = ximg[:, m, :]
        for d in range(1, n_col):
            img_copy(d).start()
        sent = img_t.at[pl.ds(0, (n_col - 1) * mi)]
        drains.append((None, [to(sent, sent, is_send.at[0], is_recv.at[0], p, sibling).wait_send]))

    def collect_image():
        for k in range(2):
            when(p != k, to(vbuf.at[k], vbuf.at[k], v_send.at[0], v_recv.at[k], p, sibling).wait_recv)
        x0 = vbuf[0]
        pad = jnp.zeros((8 - mi, width), F32)
        v1 = vbuf[1] - thin(stack(jnp.concatenate([x0, pad], axis=0)), l10[0], l10[1], NT)[0:mi]
        y0, y1 = ycut[0, q], ycut[1, q]
        wide = jnp.zeros((8 - mi, 2 * width), F32)

        def padded(g0, g1):
            return stack(jnp.concatenate([jnp.concatenate([g0, g1], axis=1), wide], axis=0))

        pair = padded(y0 - x0, y1 - v1)
        n = rows * width // 2
        fix = jnp.concatenate([thin(pair, lh[x:x + n, :], ll[x:x + n, :], NT) for x in (0, n)], axis=1)
        g0 = y0 - jnp.where(p > 0, x0, 0.0)
        g1 = y1 - jnp.where(p > 1, v1, 0.0)
        fh, fl = split(first[...])
        head_fix = thin(padded(g0, g1), fh, fl, NT)
        total = img_t[pl.ds(q * mi, mi)]
        for d in range(1, n_col):
            peer = (q + d) % n_col
            to(img_r.at[peer], img_r.at[peer], is_send.at[d], is_recv.at[peer], p, peer).wait_recv()
            total = total + img_r[peer]
        for a in range(rows):
            change = head_fix if a == 0 else fix[:, a * width:(a + 1) * width]
            image[a] = (total[:, a, :] + change[0:mi]) * scale

    def update(c):
        row_arrive(c)
        row_arrive(c + 1)
        u0 = jnp.concatenate([rowbuf[0, x] * rexp[0, x:x + 1, :] for x in (c, c + 1)], axis=1)
        u1 = jnp.concatenate([rowbuf[1, x] * rexp[1, x:x + 1, :] for x in (c, c + 1)], axis=1)
        h0, l0 = split(u0)
        h1, l1 = split(u1 - mul3(l10[0], l10[1], h0, l0))
        uh[0:width, :] = h0
        ul[0:width, :] = l0
        uh[width:, :] = h1
        ul[width:, :] = l1
        n = rows // 2
        for s in range(2):
            lo = s * n * width
            change = mul3(lh[lo:lo + n * width, :], ll[lo:lo + n * width, :], uh[...], ul[...])
            for t in range(n):
                a = s * n + t
                for e in range(2):
                    value = fact[a, c + e] * flags[c + e, a].astype(F32)
                    value = value - change[t * width:(t + 1) * width, e * width:(e + 1) * width]
                    if c + e == 0:
                        value = jnp.where(head, fact[a, 0], value)
                    fact[a, c + e] = value

        store_copy(c).start()

    def store_copy(c):
        part = pl.ds(c, 2)
        return pltpu.make_async_copy(fact.at[:, part], done_fact.at[:, part], store.at[c // 2])

    ring_end = half - 1 + 2 * (chips - 1)
    row_end = 2 * cols + lag
    steps = []

    def flush():
        for cond, fs in drains:
            if cond is None:
                for f in fs:
                    f()
            else:
                when(cond, *fs)
        drains.clear()

    done = [0]

    def tick(k):
        def ring_tick():
            ring_step(k)
            corner_step(k)
        steps.append(ring_tick)
        pass_row()

    def pass_row(count=1):
        for _ in range(count):
            if done[0] < row_end:
                steps.append(functools.partial(row_step, done[0]))
                done[0] += 1

    def work(f, *args):
        steps.append(functools.partial(f, *args))

    first_form = corner_end
    late = max(ring_end, corner_end) + 1
    for k in range(late - 1):
        tick(k)
        if k in (4, 8, 11):
            pass_row()
        if k == 0:
            work(start_flags)
        if k < 4:
            work(piece_back, k)
        if k == 3:
            work(send_s)
        if k == met + 1:
            work(early(form_flags, early_y))
        if k == met + 2:
            work(early(early_sum))
        if k == met + 3:
            work(only(p > 1, finish_back))
        if k == met + 5:
            work(flush)
            work(send_y)
        if k == met + 6:
            work(gather_s)
    drains.append((head, [t_copy().wait_send]))
    drains.append((head & (core * n_row + p != q), [yp_copy().wait_send]))
    work(take_y)
    work(piece_image, 0)
    work(send_x0)
    pass_row()
    work(only(jnp.logical_not(head), form_flags))
    work(solve_z)
    work(form, 0)
    work(form, 1)
    tick(late - 1)
    work(form, 2)
    for g in range(1, 4):
        pass_row()
        work(piece_image, g)
    work(send_image)
    pass_row()
    work(only(p < 2, finish_back))
    sent_back = back_t.at[pl.ds(0, (n_row - 1) * mb)]
    drain_back = to(sent_back, sent_back, bs_send.at[0], bs_recv.at[0], p, sibling).wait_send
    pass_row()
    work(form, 3)
    pass_row()
    work(update, 0)
    pass_row(row_end)
    for c in range(2, cols - 2, 2):
        work(update, c)
        if c == 2:
            work(send_v)
    work(only(p == last, collect_image))
    work(update, cols - 2)
    work(collect_back)
    work(only(p != last, collect_image))
    for step in steps:
        step()

    drain_back()
    flush()
    for c in range(0, cols, 2):
        store_copy(c).wait()
    whole = colbuf.at[core, pl.ds(0, rows)]
    to(whole, whole, sib_send.at[0], sib_recv.at[0], p, sibling).wait_send()
    for block in range(rows - 2 * depth, rows):
        when(head, ring(block, after).wait_send)
    part = colbuf.at[core, pl.ds(0, half)]
    for x, stop in enumerate((chips - 1, 1)):
        when((pos != 0) & (pos != stop), to(part, part, ring_send.at[x], ring_recv.at[0], p, after).wait_send)

    def row_drain(k, sems):
        for cond, ref in ((head, rowbuf.at[k, pl.ds(1, cols - 1)]), (q >= 2, rowbuf.at[k])):
            when(cond, to(ref, ref, sems.at[k, 0], row_recv.at[k, 0], up, q).wait_send)

    when(p == 1, lambda: row_drain(1, row_down))
    when((p == 0) | ((p > 0) & (p < last)), lambda: row_drain(0, row_up))
    when((p > 0) & (p < last), lambda: row_drain(1, row_up))


def store_kernel(fact, y, z, img, bck, out, y_out, z_out, img_out, bck_out, sems):
    parts = 8
    n = fact.shape[0] // parts
    copies = [
        pltpu.make_async_copy(fact.at[pl.ds(i * n, n)], out.at[pl.ds(i * n, n)], sems.at[i]) for i in range(parts)
    ]
    for i, (src, dst) in enumerate(((y, y_out), (z, z_out), (img, img_out), (bck, bck_out))):
        copies.append(pltpu.make_async_copy(src, dst, sems.at[parts + i]))
    for copy in copies:
        copy.start()
    for copy in copies:
        copy.wait()


def shards(trace, fill, pivots, direct_rhs, adjoint_rhs):
    n_row, n_col = lax.axis_size("row"), lax.axis_size("col")
    rows, cols, width = trace.shape[0], trace.shape[2], trace.shape[4]
    modes = direct_rhs.shape[2]
    blocks = trace.reshape(rows, cols, width, width)
    flags = fill.reshape(rows, cols).T
    mi, mb = modes // n_col, modes // n_row
    hbm = pl.BlockSpec(memory_space=pltpu.HBM)
    vmem = pl.BlockSpec(memory_space=pltpu.VMEM)
    shape = jax.ShapeDtypeStruct
    dma = pltpu.SemaphoreType.DMA
    V = pltpu.VMEM
    outs = pl.pallas_call(
        functools.partial(comm_kernel, n_row, n_col),
        out_shape=(
            shape((rows, cols, width, width), F32),
            shape((rows, modes, width), F32),
            shape((rows, modes, width), F32),
            shape((rows, mi, width), F32),
            shape((cols, mb, width), F32),
        ),
        in_specs=[hbm] * 5,
        out_specs=[pl.BlockSpec(memory_space=pl.ANY)] + [vmem] * 4,
        scratch_shapes=[
            V((rows, cols, width, width), F32),
            V((2, rows + 1, width, width), F32),
            V((2, cols, width, width), F32),
            V((2, 2, modes, width), F32),
            V((rows, modes, width), F32),
            V((rows, modes, width), F32),
            V((2, width, width), F32),
            pltpu.SMEM((cols, rows), jnp.int32),
            V((2, cols, rows), jnp.int32),
            V((2, cols, rows), jnp.int32),
            V((2, cols, rows), jnp.int32),
            V((2, rows, width), F32),
            V((2, cols, width), F32),
            V((rows * width, cols * width), BF16),
            V((rows * width, cols * width), BF16),
            V((rows * width, 2 * width), BF16),
            V((rows * width, 2 * width), BF16),
            V((2 * width, 2 * width), BF16),
            V((2 * width, 2 * width), BF16),
            V((4, width, width), BF16),
            V((4, width, width), BF16),
            V((2, width, width), BF16),
            V((2 * width, 2 * width), BF16),
            V((2 * width, 2 * width), BF16),
            V((width, 2 * width), F32),
            V((2 * modes, rows * width), BF16),
            V((2 * modes, cols * width), BF16),
            V((2 * modes, 2 * width), BF16),
            V((2, modes, width), F32),
            V((cols, modes, width), F32),
            V((cols, modes, width), F32),
            V((cols, modes, width), F32),
            V((cols, modes, width), F32),
            V((2, n_col, mi, width), F32),
            V((modes, cols * width), F32),
            V((modes, width), F32),
            V((n_row, modes, width), F32),
            V((modes, width), F32),
            V((modes, width), F32),
            V((3, modes, width), F32),
            V((rows, modes, width), F32),
            V((n_col, mi, width), F32),
            V((n_col, mi, width), F32),
            V((mi, width), F32),
            V((2, mi, width), F32),
            V((modes, rows, width), F32),
            V((n_col, mi, rows, width), F32),
            V((modes, cols, width), F32),
            V((n_row, mb, cols, width), F32),
            dma((cols // 2,)), dma((4,)), dma((11,)),
            dma((n_col,)), dma((2,)), dma((n_row,)), dma((2,)), dma((2, n_row)), dma((2, 2)),
            dma((n_row,)), dma, dma((n_col,)), dma((2,)), dma((3,)), dma((2,)),
            dma((rows,)), dma((rows,)), dma((rows,)), dma((rows,)),
            dma((2, cols)), dma((2, cols)), dma((2, cols)),
            dma((2,)), dma((n_row,)), dma, dma, dma((n_col,)), dma, dma((n_row,)), dma, dma, dma, dma, dma,
            dma((n_col,)), dma((n_col,)), dma((n_row,)), dma((2,)),
            dma((n_col,)), dma((n_col,)), dma((n_row,)), dma((n_row,)),
        ],
        compiler_params=pltpu.CompilerParams(
            collective_id=0, has_side_effects=True, vmem_limit_bytes=40 * 1024 * 1024
        ),
    )(*[pltpu.with_memory_space_constraint(x, pltpu.HBM) for x in (blocks, flags, pivots, direct_rhs[:, 0], adjoint_rhs[:, 0])])
    factored, direct, adjoint, image, back = pl.pallas_call(
        store_kernel,
        out_shape=tuple(shape(x.shape, F32) for x in outs),
        in_specs=[pl.BlockSpec(memory_space=pl.ANY)] + [vmem] * 4,
        out_specs=[hbm] * 5,
        scratch_shapes=[dma((12,))],
        compiler_params=pltpu.CompilerParams(vmem_limit_bytes=16 * 1024 * 1024),
    )(*outs)
    return (
        factored[:, None, :, None],
        direct[:, None],
        adjoint[:, None],
        image[:, None],
        back[:, None],
    )


def solution(mesh):
    placed = (
        P(None, "row", None, "col", None, None),
        P(None, "row", None, "col"),
        P(),
        P(None, "row", None, None),
        P(None, "row", None, None),
    )
    return jax.shard_map(
        shards,
        mesh=mesh,
        in_specs=placed,
        out_specs=(
            P(None, "row", None, "col", None, None),
            P(None, "row", None, None),
            P(None, "row", None, None),
            P(None, "row", "col", None),
            P(None, "col", "row", None),
        ),
        check_vma=False,
    )
```
